256 devices in a mesh: seq: 32 (over z, y), tp: 8 (over x, core).
Axes of the slice: x: 4, y: 4, z: 8, core: 2. Of those that a mesh axis runs over, the one named last changes fastest.
Arguments:
- query_rows: bfloat16 [8192, 6144], P('seq', 'tp'), may hold values from -6 to 6
- key_rows: bfloat16 [8192, 6144], P('seq', 'tp'), may hold values from -6 to 6
- value_rows: bfloat16 [8192, 6144], P('seq', 'tp'), may hold values from -81 to 81
- out_grad: bfloat16 [8192, 6144], P('seq'), may hold values from -6 to 6
- out_weight: bfloat16 [6144, 6144], P('tp', 'seq'), may hold values from -0.078125 to 0.078125
Outputs:
- query_grad: bfloat16 [8192, 6144], P('seq', 'tp')
- key_grad: bfloat16 [8192, 6144], P('seq', 'tp')
- value_grad: bfloat16 [8192, 6144], P('seq', 'tp')
- weight_grad: bfloat16 [6144, 6144], P('tp', 'seq')
The draws below stay inside these ranges and needn't reach their ends.
All inputs are finite; a program needn't handle non-finite values.
Results may differ from the reference program's by a relative error of at most 0.025.
Values may be sent and summed in bfloat16 or wider, within the bound.
A program may use at most 128 MiB of HBM per device.

```python
import math
import jax
import jax.numpy as jnp
from jax import lax

D = 6144
HEADS = 64
HDIM = 96
TOK_DEV = 256
TOKENS = 8192


def draw_value_rows(key, part):
    key_cols = jax.random.fold_in(key, 11)
    key_rows = jax.random.fold_in(key, 12)
    key_vals = jax.random.fold_in(key, 13)
    col_scale = jnp.exp(jax.random.uniform(key_cols, (1, HEADS * HDIM), jnp.float32) * math.log(10.0))
    row_scale = jnp.exp(jax.random.uniform(key_rows, (TOKENS, 1), jnp.float32, -0.69, 0.69))
    raw_values = jnp.clip(jax.random.normal(key_vals, (TOKENS, HEADS * HDIM), jnp.float32), -4.0, 4.0)
    return (raw_values * col_scale * row_scale).astype(jnp.bfloat16)


def spiked(result, rng, source, target, shards_of, factor):
    def block_of(dim):
        return (jnp.arange(result.shape[dim]) // (result.shape[dim] // shards_of)).reshape((-1,) + (1,) * (result.ndim - 1 - dim))

    near = jax.random.permutation(rng, shards_of)[block_of(target)]
    other_side = (block_of(target) + shards_of // 2) % shards_of
    return jnp.where((block_of(source) == near) | (block_of(source) == other_side), factor * result, result)


def level_of(key, extent, cuts, smallest, high):
    loudness = 1.0
    for position, shards_of in cuts:
        heights = jax.random.uniform(jax.random.fold_in(jax.random.fold_in(key, 6), position), (shards_of,), jnp.float32, smallest / len(cuts), high / len(cuts))
        loudness = loudness * jnp.repeat(jnp.exp(heights), extent[position] // shards_of).reshape((-1,) + (1,) * (len(extent) - 1 - position))
    return loudness


def centred(own_key, extent, spread, limit, split=(), kind=jnp.bfloat16):
    array = jax.random.normal(own_key, extent, jnp.float32) * spread
    if len(split) > 0:
        array = level_of(own_key, extent, split, -0.22, 0.18) * array
    return jnp.clip(array, min=-limit, max=limit).astype(kind)


def gaussian_with(stream_key, dims, deviation, limit, cuts, heavy, held_as=jnp.bfloat16):
    entries = deviation * jax.random.normal(stream_key, dims, jnp.float32)
    if cuts:
        entries = entries * level_of(stream_key, dims, cuts, -0.22, 0.18)
    return jnp.clip(spiked(entries, jax.random.fold_in(stream_key, 3), *heavy), -limit, limit).astype(held_as)


def setup_inputs(seed: int = 0) -> dict:
    key_of = jax.random.split(jax.random.key(seed), 6)
    return {
        "query_rows": centred(key_of[0], (TOKENS, HEADS * HDIM), 1.0, 6.0, ((0, 32), (1, 8))),
        "key_rows": centred(key_of[1], (TOKENS, HEADS * HDIM), 1.0, 6.0, ((0, 32), (1, 8))),
        "value_rows": draw_value_rows(jax.random.fold_in(key_of[5], 71), 0),
        "out_grad": gaussian_with(key_of[3], (TOKENS, D), 1.0, 6.0, ((0, 32),), (0, 1, 32, 2.75)),
        "out_weight": centred(key_of[4], (HEADS * HDIM, D), (HEADS * HDIM) ** -0.5, 0.078125, ((0, 8), (1, 32))),
    }


EPSILON = 1e-06

def reference(query_rows, key_rows, value_rows, out_grad, out_weight):
    blocks = TOKENS // TOK_DEV
    all_columns = HEADS * HDIM
    highest = lax.Precision.HIGHEST

    def by_head(matrix):
        return matrix.reshape(blocks, TOK_DEV, HEADS, HDIM)
    queries = by_head(query_rows)
    keyset = by_head(key_rows)
    valueset = by_head(value_rows)
    causal = jnp.tril(jnp.ones((TOK_DEV, TOK_DEV), jnp.float32))

    def forward(running, inputs):
        query_f32 = inputs[0].astype(jnp.float32)
        key_f32 = inputs[1].astype(jnp.float32)
        value_f32 = inputs[2].astype(jnp.float32)
        scores = (jnp.einsum('thd,shd->hts', query_f32, key_f32) * causal).astype(jnp.bfloat16)
        attended = jnp.einsum('hts,she->the', scores.astype(jnp.float32), value_f32)
        attended = attended + jnp.einsum('thd,hde->the', query_f32, running, precision=highest)
        updated = running + jnp.einsum('shd,she->hde', key_f32, value_f32, precision=highest)
        return (updated, (attended, running))
    start_state = jnp.zeros((HEADS, HDIM, HDIM), jnp.float32)
    _, (attended, prefix_state) = lax.scan(forward, start_state, (queries, keyset, valueset))
    attended = attended.reshape(TOKENS, all_columns)
    normed_grad = lax.dot_general(out_grad, out_weight, (((1,), (1,)), ((), ())), preferred_element_type=jnp.float32)
    row_rms = jnp.sqrt(lax.optimization_barrier(jnp.sum(attended * attended, axis=1)) / all_columns + EPSILON)
    normed = attended / row_rms[:, None]
    normed_bf = normed.astype(jnp.bfloat16)
    normed_blocks = normed_bf.reshape(blocks, TOK_DEV, all_columns)
    grad_blocks = out_grad.reshape(blocks, TOK_DEV, D)

    def add_block(running, inputs):
        partial_term = lax.dot_general(inputs[0], inputs[1], (((0,), (0,)), ((), ())), preferred_element_type=jnp.float32)
        rounded = lax.optimization_barrier(partial_term.astype(jnp.bfloat16))
        return (running + rounded.astype(jnp.float32), None)
    weight_sum, _ = lax.scan(add_block, jnp.zeros((all_columns, D), jnp.float32), (normed_blocks, grad_blocks))
    weight_grad = weight_sum.astype(jnp.bfloat16)
    cross = lax.optimization_barrier(jnp.sum(normed_grad * attended, axis=1)) / row_rms
    attended_grad = ((normed_grad - normed * (cross / all_columns)[:, None]) / row_rms[:, None]).astype(jnp.bfloat16)
    grad_heads = by_head(attended_grad)

    def backward(running, inputs):
        query_f32 = inputs[0].astype(jnp.float32)
        key_f32 = inputs[1].astype(jnp.float32)
        value_f32 = inputs[2].astype(jnp.float32)
        grad_f32 = inputs[3].astype(jnp.float32)
        earlier = inputs[4]
        scores = (jnp.einsum('thd,shd->hts', query_f32, key_f32) * causal).astype(jnp.bfloat16).astype(jnp.float32)
        score_grad = (jnp.einsum('the,she->hts', grad_f32, value_f32) * causal).astype(jnp.bfloat16).astype(jnp.float32)
        query_grad = jnp.einsum('hts,shd->thd', score_grad, key_f32)
        query_grad = query_grad + jnp.einsum('the,hde->thd', grad_f32, earlier, precision=highest)
        key_grad = jnp.einsum('hts,thd->shd', score_grad, query_f32)
        key_grad = key_grad + jnp.einsum('she,hde->shd', value_f32, running, precision=highest)
        value_grad = jnp.einsum('hts,the->she', scores, grad_f32)
        value_grad = value_grad + jnp.einsum('shd,hde->she', key_f32, running, precision=highest)
        updated = running + jnp.einsum('thd,the->hde', query_f32, grad_f32, precision=highest)
        return (updated, (query_grad.astype(jnp.bfloat16), key_grad.astype(jnp.bfloat16), value_grad.astype(jnp.bfloat16)))
    _, (query_grad, key_grad, value_grad) = lax.scan(backward, start_state, (queries, keyset, valueset, grad_heads, prefix_state), reverse=True)
    return (query_grad.reshape(TOKENS, all_columns), key_grad.reshape(TOKENS, all_columns), value_grad.reshape(TOKENS, all_columns), weight_grad)
```

```python
import jax
import jax.numpy as jnp
from jax import lax
from jax.experimental import pallas as pl
from jax.experimental.pallas import tpu as pltpu
from jax.sharding import PartitionSpec as P

HDIM = 96
EPSILON = 1e-06
NY, NZ, NT = 4, 8, 8
TOK = 256
COLS = 768
GROUP = 384
CHUNK = 192
HALF = 96
QUARTER = 48
MODEL = 6144
WINDOWS = ((0, 128), (0, 256), (128, 384), (256, 384))
SEMS = 120
F32 = jnp.float32
BF16 = jnp.bfloat16


def dot(a, b, ca, cb):
    return lax.dot_general(a, b, (((ca,), (cb,)), ((), ())), preferred_element_type=F32)


def head_mask(h, lo, hi):
    lane = lax.broadcasted_iota(jnp.int32, (1, hi - lo), 1) + lo
    inside = (lane >= HDIM * h) & (lane < HDIM * (h + 1))
    return jnp.where(inside, 1.0, 0.0).astype(F32)


def kernel(
    q, k, v, w, og, qg, kg, vg, dw,
    grads, weights, normed, scores, att, ng, part, psend, precv, hsend, hrecv,
    lstate, lrecv, tsend, trecv, tacc, pfs, state, blocks, ssend, srecv,
    own, dsend, drecv, dob, gh, send, recv, lsem,
):
    s, t = lax.axis_index("seq"), lax.axis_index("tp")
    z, y = s // NY, s % NY
    core = t % 2
    odd = y % 2
    right, left, twin = (t + 2) % NT, (t + NT - 2) % NT, t + 1 - 2 * core
    count = [0]
    started = []

    def along_y(d):
        return z * NY + (y + d) % NY

    def along_z(d):
        return ((z + d + NZ) % NZ) * NY + y

    def copy(src, dst, seq, tp):
        i = count[0]
        count[0] += 1
        return pltpu.make_async_remote_copy(
            src_ref=src, dst_ref=dst, send_sem=send.at[i], recv_sem=recv.at[i],
            device_id={"seq": seq, "tp": tp}, device_id_type=pl.DeviceIdType.MESH,
        )

    def go(c):
        c.start()
        started.append(c)

    barrier = pltpu.get_barrier_semaphore()
    peers = [(along_y(d), t) for d in range(1, NY)]
    peers += [(along_z(d), t) for d in range(1, NZ)]
    peers += [(s, (t + d) % NT) for d in range(1, NT)]
    for seq, tp in peers:
        pl.semaphore_signal(
            barrier, inc=1, device_id={"seq": seq, "tp": tp}, device_id_type=pl.DeviceIdType.MESH
        )

    def window(at_z, at_y):
        return pl.multiple_of(COLS * at_z + GROUP * (at_y // 2) + 128 * (at_y % 2), 128)

    own_grads = []
    for j in range(NZ):
        c = pltpu.make_async_copy(
            og.at[:, pl.ds(window(j, y), 256)],
            grads.at[pl.ds(0, TOK), pl.ds(256 * j, 256)],
            lsem.at[j],
        )
        c.start()
        own_grads.append(c)

    for j in range(NZ):
        pad = pl.multiple_of(256 * j + CHUNK * (1 - odd), 64)
        weights[pl.ds(pad, 64), :] = jnp.zeros((64, COLS), BF16)

    def weight_rows(j, h, n):
        return pl.ds(pl.multiple_of(256 * j + 64 * odd + HALF * h, 32), n)

    weights[weight_rows(z, 0, CHUNK), :] = w[...].T

    pl.semaphore_wait(barrier, len(peers))

    wcopy = {}
    for step in range(4):
        for way in (0, 1):
            j = (z + NZ - step) % NZ if way == 0 else (z + step) % NZ
            for h in (0, 1):
                if step < 3 or h == way:
                    rows = weight_rows(j, h, HALF)
                    wcopy[step, way, h] = copy(
                        weights.at[rows], weights.at[rows], along_z(1 - 2 * way), t
                    )
    acopy = {}
    for d in range(1, NY):
        acopy[d] = copy(
            og.at[:, pl.ds(window(t, (y + d) % NY), 256)],
            grads.at[pl.ds(TOK * (NY - d), TOK), pl.ds(pl.multiple_of(256 * t, 256), 256)],
            along_y(d), t,
        )
    bcopy = {}
    for r in range(1, NY):
        def piece(at_t, half=None):
            rows = pl.ds(TOK * r, TOK) if half is None else pl.ds(TOK * r + 128 * half, 128)
            return grads.at[rows, pl.ds(pl.multiple_of(256 * at_t, 256), 256)]

        for name, tp, at_t, half in (
            ("right", right, t, None),
            ("left", left, t, None),
            ("twin", twin, t, None),
            ("far_right", right, left, 0),
            ("far_left", left, right, 1),
            ("twin_left", twin, left, None),
            ("twin_right", twin, right, None),
            ("twin_far0", twin, (t + 4) % NT, 0),
            ("twin_far1", twin, (t + 4) % NT, 1),
        ):
            bcopy[r, name] = copy(piece(at_t, half), piece(at_t, half), s, tp)

    for h in (0, 1):
        for way in (0, 1):
            go(wcopy[0, way, h])
    for d in range(1, NY):
        go(acopy[d])

    def weight_step(step):
        for h in (0, 1):
            for way in (0, 1):
                if (step, way, h) in wcopy:
                    wcopy[step, way, h].wait_recv()
                    if (step + 1, way, h) in wcopy:
                        go(wcopy[step + 1, way, h])

    def local_state(a, b, slot):
        for g in range(2):
            full = dot(a[:, GROUP * g : GROUP * (g + 1)], b[:, GROUP * g : GROUP * (g + 1)], 0, 0)
            kept = jnp.zeros((HDIM, GROUP), F32)
            for h in range(4):
                kept = kept + full[HDIM * h : HDIM * (h + 1), :] * head_mask(h, 0, GROUP)
            lstate[slot, HDIM * g : HDIM * (g + 1), :] = kept.astype(BF16)

    states = []
    for slot in (0, 1):
        sign = 1 - 2 * slot
        first = [
            copy(
                lstate.at[slot, pl.ds(pl.multiple_of(QUARTER * ((y + d) % NY), 16), QUARTER)],
                lrecv.at[slot, y], along_y(d), t,
            )
            for d in range(1, NY)
        ]
        second = [
            copy(tsend.at[slot], trecv.at[slot, z], along_z(sign * d), t) for d in range(1, NZ)
        ]
        third = [
            copy(
                pfs.at[slot, (y + d) % NY],
                state.at[slot, pl.ds(pl.multiple_of(QUARTER * y, 16), QUARTER)],
                along_y(d), t,
            )
            for d in range(1, NY)
        ]
        states.append((first, second, third))

    def state_first(slot):
        for c in states[slot][0]:
            go(c)
        mine = pl.ds(pl.multiple_of(QUARTER * y, 16), QUARTER)
        lrecv[slot, y] = lstate[slot, mine, :]

    def state_second(slot):
        for c in states[slot][0]:
            c.wait_recv()
        total = lrecv[slot, 0].astype(F32)
        for j in range(1, NY):
            total = total + lrecv[slot, j].astype(F32)
        tsend[slot] = total.astype(BF16)
        for d in range(1, NZ):
            reaches = z + d < NZ if slot == 0 else z >= d

            @pl.when(reaches)
            def _():
                states[slot][1][d - 1].start()

    def state_third(slot):
        tacc[...] = jnp.zeros((QUARTER, GROUP), F32)
        for d in range(1, NZ):
            comes = z >= d if slot == 0 else z + d < NZ
            source = z - d if slot == 0 else z + d

            @pl.when(comes)
            def _():
                states[slot][1][d - 1].wait_recv()
                tacc[...] += trecv[slot, source].astype(F32)

        running = tacc[...]
        for j in range(NY) if slot == 0 else reversed(range(NY)):
            pfs[slot, j] = running.astype(BF16)
            running = running + lrecv[slot, j].astype(F32)
        for c in states[slot][2]:
            go(c)
        mine = pl.ds(pl.multiple_of(QUARTER * y, 16), QUARTER)
        state[slot, mine, :] = pfs[slot, y]

    def state_last(slot):
        for c in states[slot][2]:
            c.wait_recv()
        for g in range(2):
            compact = state[slot, HDIM * g : HDIM * (g + 1), :]
            for h in range(4):
                blocks[slot, g, HDIM * h : HDIM * (h + 1), :] = compact * head_mask(
                    h, 0, GROUP
                ).astype(BF16)

    sums = [
        [copy(ssend.at[i], srecv.at[i, d - 1], s, (t + d) % NT) for d in range(1, NT)]
        for i in range(2)
    ]

    def sum_send(i, column):
        ssend[i] = jnp.broadcast_to(column, (TOK, 128)).T[:8]
        for c in sums[i]:
            go(c)

    def sum_wait(i):
        total = ssend[i]
        for d in range(1, NT):
            sums[i][d - 1].wait_recv()
            total = total + srecv[i, d - 1]
        return jnp.broadcast_to(total[:1], (128, TOK)).T[:, :1]

    local_state(k, v, 0)
    state_first(0)

    rows = lax.broadcasted_iota(jnp.int32, (TOK, TOK), 0)
    columns = lax.broadcasted_iota(jnp.int32, (TOK, TOK), 1)

    def lanes(g, lo, hi):
        return pl.ds(pl.multiple_of(GROUP * g + lo, 128), hi - lo)

    def forward(g):
        att[:, lanes(g, 0, GROUP)] = jnp.zeros((TOK, GROUP), F32)
        for h, (lo, hi) in enumerate(WINDOWS):
            mask = head_mask(h, lo, hi).astype(BF16)
            at = lanes(g, lo, hi)
            score = dot(q[:, at], k[:, at] * mask, 1, 1)
            score = jnp.where(rows >= columns, score, 0.0).astype(BF16)
            scores[4 * g + h] = score
            att[:, at] += dot(score, v[:, at] * mask, 1, 0)

    forward(0)
    state_second(0)
    weight_step(0)
    for d in range(1, NY):
        acopy[d].wait_recv()
        for name in ("right", "left", "twin"):
            go(bcopy[NY - d, name])
    forward(1)
    state_third(0)
    weight_step(1)
    for r in range(1, NY):
        bcopy[r, "right"].wait_recv()
        go(bcopy[r, "far_right"])
        go(bcopy[r, "twin_left"])
        bcopy[r, "left"].wait_recv()
        go(bcopy[r, "far_left"])
        go(bcopy[r, "twin_right"])
    state_last(0)
    for g in range(2):
        at = lanes(g, 0, GROUP)
        att[:, at] += dot(q[:, at], blocks[0, g], 1, 0)
    attended = att[...]
    sum_send(0, jnp.sum(attended * attended, axis=1, keepdims=True))
    weight_step(2)
    for r in range(1, NY):
        bcopy[r, "far_right"].wait_recv()
        go(bcopy[r, "twin_far0"])
        bcopy[r, "far_left"].wait_recv()
        go(bcopy[r, "twin_far1"])
    inverse = 1.0 / jnp.sqrt(sum_wait(0) / MODEL + EPSILON)
    normed[pl.ds(0, TOK), :] = (att[...] * inverse).astype(BF16)

    ncopy = {
        "up": copy(normed.at[pl.ds(0, TOK)], normed.at[pl.ds(3 * TOK, TOK)], along_y(1), t),
        "down": copy(normed.at[pl.ds(0, TOK)], normed.at[pl.ds(TOK, TOK)], along_y(3), t),
        "far_up": copy(
            normed.at[pl.ds(3 * TOK, 128)], normed.at[pl.ds(2 * TOK, 128)], along_y(1), t
        ),
        "far_down": copy(
            normed.at[pl.ds(TOK + 128, 128)], normed.at[pl.ds(2 * TOK + 128, 128)], along_y(3), t
        ),
    }
    go(ncopy["up"])
    go(ncopy["down"])

    weight_step(3)
    for name in ("twin", "twin_left", "twin_right", "twin_far0", "twin_far1"):
        for r in range(1, NY):
            bcopy[r, name].wait_recv()
    for c in own_grads:
        c.wait()

    def product(r):
        @pl.loop(0, 3)
        def _(n):
            at = pl.ds(pl.multiple_of(256 * n, 256), 256)
            part[:, at] = dot(grads[pl.ds(TOK * r, TOK), :], weights[:, at], 1, 0)

    half_up = copy(hsend.at[pl.ds(0, 128)], hrecv.at[0], along_y(1), t)
    half_down = copy(hsend.at[pl.ds(128, 128)], hrecv.at[1], along_y(3), t)
    product(2)
    hsend[...] = part[...].astype(BF16)
    go(half_up)
    go(half_down)
    pcopy = {}
    for i, d in enumerate((1, 3)):
        for h in (0, 1):
            at = pl.ds(128 * h, 128)
            pcopy[i, h] = copy(psend.at[i, at], precv.at[i, at], along_y(d), t)
    product(1)
    psend[0, 128:] = part[128:].astype(BF16)
    go(pcopy[0, 1])
    half_up.wait_recv()
    psend[0, :128] = (part[:128] + hrecv[0].astype(F32)).astype(BF16)
    go(pcopy[0, 0])
    product(3)
    psend[1, :128] = part[:128].astype(BF16)
    go(pcopy[1, 0])
    half_down.wait_recv()
    psend[1, 128:] = (part[128:] + hrecv[1].astype(F32)).astype(BF16)
    go(pcopy[1, 1])
    ncopy["up"].wait_recv()
    go(ncopy["far_up"])
    ncopy["down"].wait_recv()
    go(ncopy["far_down"])
    product(0)

    def chunk(off):
        j = (z + off) % NZ
        turned = grads[:, pl.ds(pl.multiple_of(256 * j, 256), 256)].T
        dob[...] = turned

        @pl.loop(0, 3)
        def _(n):
            at = pl.ds(pl.multiple_of(256 * n, 256), 256)
            own[off, :, at] = dot(dob[...], normed[:, at], 1, 0)

    def valid(off, h):
        return own[off, pl.ds(pl.multiple_of(64 * odd + HALF * h, 32), HALF), :]

    dcopy = {}
    for step in range(4):
        for way in (0, 1):
            for h in (0, 1):
                if step > 0 or h == way:
                    at = pl.ds(HALF * h, HALF)
                    dcopy[step, way, h] = copy(
                        dsend.at[way, step, at], drecv.at[way, step, at],
                        along_z(2 * way - 1), t,
                    )

    ncopy["far_up"].wait_recv()
    ncopy["far_down"].wait_recv()
    chunk(4)
    for way in (0, 1):
        dsend[way, 0, HALF * way : HALF * (way + 1), :] = valid(4, way).astype(BF16)
        go(dcopy[0, way, way])

    @pl.loop(0, 7)
    def _(i):
        e = i % 2
        chunk((1 - e) * (3 - i // 2) + e * (5 + i // 2))

    def grad_step(step):
        for h in (0, 1):
            for way in (0, 1):
                off = NZ - 4 + step if way == 0 else 4 - step
                total = valid(off, h)
                if (step - 1, way, h) in dcopy:
                    dcopy[step - 1, way, h].wait_recv()
                    got = drecv[way, step - 1, HALF * h : HALF * (h + 1), :]
                    total = total + got.astype(F32)
                dsend[way, step, HALF * h : HALF * (h + 1), :] = total.astype(BF16)
                go(dcopy[step, way, h])

    for c in pcopy.values():
        c.wait_recv()
    ng[...] = part[...] + precv[0].astype(F32) + precv[1].astype(F32)
    sum_send(1, jnp.sum(ng[...] * att[...], axis=1, keepdims=True))
    grad_step(1)
    cross = sum_wait(1) * inverse
    grad_heads = (ng[...] - att[...] * (inverse * cross / MODEL)) * inverse
    gh[...] = grad_heads.astype(BF16)
    local_state(q, gh, 1)
    state_first(1)

    def backward(g):
        at = lanes(g, 0, GROUP)
        att[:, at] = dot(gh[:, at], blocks[0, g], 1, 1)
        part[:, at] = jnp.zeros((TOK, GROUP), F32)
        ng[:, at] = jnp.zeros((TOK, GROUP), F32)
        for h, (lo, hi) in enumerate(WINDOWS):
            mask = head_mask(h, lo, hi).astype(BF16)
            at = lanes(g, lo, hi)
            score = dot(gh[:, at], v[:, at] * mask, 1, 1)
            score = jnp.where(rows >= columns, score, 0.0).astype(BF16)
            att[:, at] += dot(score, k[:, at] * mask, 1, 0)
            part[:, at] += dot(score, q[:, at] * mask, 0, 0)
            ng[:, at] += dot(scores[4 * g + h], gh[:, at] * mask, 0, 0)

    backward(0)
    state_second(1)
    grad_step(2)
    backward(1)
    qg[...] = att[...].astype(BF16)
    state_third(1)
    grad_step(3)
    state_last(1)
    for g in range(2):
        at = lanes(g, 0, GROUP)
        kg[:, at] = (part[:, at] + dot(v[:, at], blocks[1, g], 1, 1)).astype(BF16)
        vg[:, at] = (ng[:, at] + dot(k[:, at], blocks[1, g], 1, 0)).astype(BF16)
    for h in (0, 1):
        for way in (0, 1):
            dcopy[3, way, h].wait_recv()
        at = slice(HALF * h, HALF * (h + 1))
        total = valid(0, h) + drecv[0, 3, at, :].astype(F32) + drecv[1, 3, at, :].astype(F32)
        own[1, at, :] = total
    dw[...] = own[1, :CHUNK, :].T.astype(BF16)

    for c in started:
        c.wait_send()
    for slot in (0, 1):
        for d in range(1, NZ):
            reaches = z + d < NZ if slot == 0 else z >= d

            @pl.when(reaches)
            def _():
                states[slot][1][d - 1].wait_send()


def body(*args):
    vmem = pl.BlockSpec(memory_space=pltpu.VMEM)
    block = jax.ShapeDtypeStruct((TOK, COLS), BF16)
    return pl.pallas_call(
        kernel,
        out_shape=(block, block, block, jax.ShapeDtypeStruct((COLS, CHUNK), BF16)),
        in_specs=[vmem] * 4 + [pl.BlockSpec(memory_space=pl.ANY)],
        out_specs=(vmem,) * 4,
        scratch_shapes=[
            pltpu.VMEM((NY * TOK, NZ * 256), BF16),
            pltpu.VMEM((NZ * 256, COLS), BF16),
            pltpu.VMEM((NY * TOK, COLS), BF16),
            pltpu.VMEM((8, TOK, TOK), BF16),
            pltpu.VMEM((TOK, COLS), F32),
            pltpu.VMEM((TOK, COLS), F32),
            pltpu.VMEM((TOK, COLS), F32),
            pltpu.VMEM((2, TOK, COLS), BF16),
            pltpu.VMEM((2, TOK, COLS), BF16),
            pltpu.VMEM((TOK, COLS), BF16),
            pltpu.VMEM((2, 128, COLS), BF16),
            pltpu.VMEM((2, 192, GROUP), BF16),
            pltpu.VMEM((2, NY, QUARTER, GROUP), BF16),
            pltpu.VMEM((2, QUARTER, GROUP), BF16),
            pltpu.VMEM((2, NZ, QUARTER, GROUP), BF16),
            pltpu.VMEM((QUARTER, GROUP), F32),
            pltpu.VMEM((2, NY, QUARTER, GROUP), BF16),
            pltpu.VMEM((2, 192, GROUP), BF16),
            pltpu.VMEM((2, 2, GROUP, GROUP), BF16),
            pltpu.VMEM((2, 8, TOK), F32),
            pltpu.VMEM((2, NT - 1, 8, TOK), F32),
            pltpu.VMEM((NZ, 256, COLS), F32),
            pltpu.VMEM((2, 4, CHUNK, COLS), BF16),
            pltpu.VMEM((2, 4, CHUNK, COLS), BF16),
            pltpu.VMEM((256, NY * TOK), BF16),
            pltpu.VMEM((TOK, COLS), BF16),
            pltpu.SemaphoreType.DMA((SEMS,)),
            pltpu.SemaphoreType.DMA((SEMS,)),
            pltpu.SemaphoreType.DMA((NZ,)),
        ],
        compiler_params=pltpu.CompilerParams(
            collective_id=0, has_side_effects=True, vmem_limit_bytes=56 << 20
        ),
    )(*args)


def solution(mesh):
    placed = (P("seq", "tp"), P("seq", "tp"), P("seq", "tp"), P("seq", None), P("tp", "seq"))
    inner = jax.shard_map(
        lambda q, k, v, og, w: body(q, k, v, w, og),
        mesh=mesh,
        in_specs=placed,
        out_specs=(P("seq", "tp"), P("seq", "tp"), P("seq", "tp"), P("tp", "seq")),
        check_vma=False,
    )
    return inner
```

```python
import jax
import jax.numpy as jnp
from jax import lax
from jax.experimental import pallas as pl
from jax.experimental.pallas import tpu as pltpu
from jax.sharding import PartitionSpec as P

HDIM = 96
EPSILON = 1e-06
NY, NZ, NT = 4, 8, 8
TOK = 256
COLS = 768
GROUP = 384
CHUNK = 192
HALF = 96
QUARTER = 48
MODEL = 6144
WINDOWS = ((0, 128), (0, 256), (128, 384), (256, 384))
SEMS = 120
F32 = jnp.float32
BF16 = jnp.bfloat16


def dot(a, b, ca, cb):
    return lax.dot_general(a, b, (((ca,), (cb,)), ((), ())), preferred_element_type=F32)


def head_mask(h, lo, hi):
    lane = lax.broadcasted_iota(jnp.int32, (1, hi - lo), 1) + lo
    inside = (lane >= HDIM * h) & (lane < HDIM * (h + 1))
    return jnp.where(inside, 1.0, 0.0).astype(F32)


def kernel(
    q, k, v, w, og, qg, kg, vg, dw,
    grads, weights, normed, scores, att, ng, part, psend, precv, hsend, hrecv,
    lstate, lrecv, tsend, trecv, tacc, pfs, state, blocks, ssend, srecv,
    own, dsend, drecv, turned, gh, held, send, recv, lsem,
):
    s, t = lax.axis_index("seq"), lax.axis_index("tp")
    z, y = s // NY, s % NY
    core = t % 2
    odd = y % 2
    right, left, twin = (t + 2) % NT, (t + NT - 2) % NT, t + 1 - 2 * core
    count = [0]
    started = []

    def along_y(d):
        return z * NY + (y + d) % NY

    def along_z(d):
        return ((z + d + NZ) % NZ) * NY + y

    def copy(src, dst, seq, tp):
        i = count[0]
        count[0] += 1
        return pltpu.make_async_remote_copy(
            src_ref=src, dst_ref=dst, send_sem=send.at[i], recv_sem=recv.at[i],
            device_id={"seq": seq, "tp": tp}, device_id_type=pl.DeviceIdType.MESH,
        )

    def go(c):
        c.start()
        started.append(c)

    barrier = pltpu.get_barrier_semaphore()
    peers = [(along_y(d), t) for d in range(1, NY)]
    peers += [(along_z(d), t) for d in range(1, NZ)]
    peers += [(s, (t + d) % NT) for d in range(1, NT)]
    for seq, tp in peers:
        pl.semaphore_signal(
            barrier, inc=1, device_id={"seq": seq, "tp": tp}, device_id_type=pl.DeviceIdType.MESH
        )

    def window(at_z, at_y):
        return pl.multiple_of(COLS * at_z + GROUP * (at_y // 2) + 128 * (at_y % 2), 128)

    own_grads = []
    for j in range(NZ):
        c = pltpu.make_async_copy(
            og.at[:, pl.ds(window(j, y), 256)],
            grads.at[pl.ds(0, TOK), pl.ds(256 * j, 256)],
            lsem.at[j],
        )
        c.start()
        own_grads.append(c)

    for j in range(NZ):
        pad = pl.multiple_of(256 * j + CHUNK * (1 - odd), 64)
        weights[pl.ds(pad, 64), :] = jnp.zeros((64, COLS), BF16)

    def weight_rows(j, h, n):
        return pl.ds(pl.multiple_of(256 * j + 64 * odd + HALF * h, 32), n)

    weights[weight_rows(z, 0, CHUNK), :] = w[...]

    wcopy = {}
    for step in range(4):
        for way in (0, 1):
            j = (z + NZ - step) % NZ if way == 0 else (z + step) % NZ
            for h in (0, 1):
                if step < 3 or h == way:
                    rows = weight_rows(j, h, HALF)
                    wcopy[step, way, h] = copy(
                        weights.at[rows], weights.at[rows], along_z(1 - 2 * way), t
                    )
    acopy = {}
    for d in range(1, NY):
        acopy[d] = copy(
            og.at[:, pl.ds(window(t, (y + d) % NY), 256)],
            grads.at[pl.ds(TOK * (NY - d), TOK), pl.ds(pl.multiple_of(256 * t, 256), 256)],
            along_y(d), t,
        )
    bcopy = {}
    for r in range(1, NY):
        def piece(at_t, half=None):
            rows = pl.ds(TOK * r, TOK) if half is None else pl.ds(TOK * r + 128 * half, 128)
            return grads.at[rows, pl.ds(pl.multiple_of(256 * at_t, 256), 256)]

        for name, tp, at_t, half in (
            ("right", right, t, None),
            ("left", left, t, None),
            ("twin", twin, t, None),
            ("far_right", right, left, 0),
            ("far_left", left, right, 1),
            ("twin_left", twin, left, None),
            ("twin_right", twin, right, None),
            ("twin_far0", twin, (t + 4) % NT, 0),
            ("twin_far1", twin, (t + 4) % NT, 1),
        ):
            bcopy[r, name] = copy(piece(at_t, half), piece(at_t, half), s, tp)

    def weight_step(step):
        for turn in (0, 1):
            for way in (0, 1):
                h = way ^ turn
                if (step, way, h) in wcopy:
                    wcopy[step, way, h].wait_recv()
                    if (step + 1, way, h) in wcopy:
                        go(wcopy[step + 1, way, h])

    def local_state(a, b, slot):
        for g in range(2):
            full = dot(a[:, GROUP * g : GROUP * (g + 1)], b[:, GROUP * g : GROUP * (g + 1)], 0, 0)
            kept = jnp.zeros((HDIM, GROUP), F32)
            for h in range(4):
                kept = kept + full[HDIM * h : HDIM * (h + 1), :] * head_mask(h, 0, GROUP)
            lstate[slot, HDIM * g : HDIM * (g + 1), :] = kept.astype(BF16)

    states = []
    for slot in (0, 1):
        sign = 1 - 2 * slot
        first = [
            copy(
                lstate.at[slot, pl.ds(pl.multiple_of(QUARTER * ((y + d) % NY), 16), QUARTER)],
                lrecv.at[slot, y], along_y(d), t,
            )
            for d in range(1, NY)
        ]
        second = [
            copy(tsend.at[slot], trecv.at[slot, z], along_z(sign * d), t) for d in range(1, NZ)
        ]
        third = [
            copy(
                pfs.at[slot, (y + d) % NY],
                state.at[slot, pl.ds(pl.multiple_of(QUARTER * y, 16), QUARTER)],
                along_y(d), t,
            )
            for d in range(1, NY)
        ]
        states.append((first, second, third))

    def state_first(slot):
        for c in states[slot][0]:
            go(c)
        mine = pl.ds(pl.multiple_of(QUARTER * y, 16), QUARTER)
        lrecv[slot, y] = lstate[slot, mine, :]

    def state_second(slot):
        for c in states[slot][0]:
            c.wait_recv()
        total = lrecv[slot, 0].astype(F32)
        for j in range(1, NY):
            total = total + lrecv[slot, j].astype(F32)
        tsend[slot] = total.astype(BF16)
        for d in range(1, NZ):
            reaches = z + d < NZ if slot == 0 else z >= d

            @pl.when(reaches)
            def _():
                states[slot][1][d - 1].start()

    def state_third(slot):
        tacc[...] = jnp.zeros((QUARTER, GROUP), F32)
        for d in range(1, NZ):
            comes = z >= d if slot == 0 else z + d < NZ
            source = z - d if slot == 0 else z + d

            @pl.when(comes)
            def _():
                states[slot][1][d - 1].wait_recv()
                tacc[...] += trecv[slot, source].astype(F32)

        running = tacc[...]
        for j in range(NY) if slot == 0 else reversed(range(NY)):
            pfs[slot, j] = running.astype(BF16)
            running = running + lrecv[slot, j].astype(F32)
        for c in states[slot][2]:
            go(c)
        mine = pl.ds(pl.multiple_of(QUARTER * y, 16), QUARTER)
        state[slot, mine, :] = pfs[slot, y]

    def state_last(slot):
        for c in states[slot][2]:
            c.wait_recv()
        for g in range(2):
            compact = state[slot, HDIM * g : HDIM * (g + 1), :]
            for h in range(4):
                blocks[slot, g, HDIM * h : HDIM * (h + 1), :] = compact * head_mask(
                    h, 0, GROUP
                ).astype(BF16)

    sums = [
        [copy(ssend.at[i], srecv.at[i, d - 1], s, (t + d) % NT) for d in range(1, NT)]
        for i in range(2)
    ]

    def sum_send(i, column):
        ssend[i] = jnp.broadcast_to(column, (TOK, 128)).T[:8]
        for c in sums[i]:
            go(c)

    def sum_wait(i):
        total = ssend[i]
        for d in range(1, NT):
            sums[i][d - 1].wait_recv()
            total = total + srecv[i, d - 1]
        return jnp.broadcast_to(total[:1], (128, TOK)).T[:, :1]

    local_state(k, v, 0)
    pl.semaphore_wait(barrier, len(peers))
    state_first(0)
    for turn in (0, 1):
        for way in (0, 1):
            go(wcopy[0, way, way ^ turn])
    for d in range(1, NY):
        go(acopy[d])

    rows = lax.broadcasted_iota(jnp.int32, (TOK, TOK), 0)
    columns = lax.broadcasted_iota(jnp.int32, (TOK, TOK), 1)

    def lanes(g, lo, hi):
        return pl.ds(pl.multiple_of(GROUP * g + lo, 128), hi - lo)

    def forward(g):
        att[:, lanes(g, 0, GROUP)] = jnp.zeros((TOK, GROUP), F32)
        for h, (lo, hi) in enumerate(WINDOWS):
            mask = head_mask(h, lo, hi).astype(BF16)
            at = lanes(g, lo, hi)
            score = dot(q[:, at], k[:, at] * mask, 1, 1)
            score = jnp.where(rows >= columns, score, 0.0).astype(BF16)
            scores[4 * g + h] = score
            att[:, at] += dot(score, v[:, at] * mask, 1, 0)

    forward(0)
    state_second(0)
    weight_step(0)
    for d in range(1, NY):
        acopy[d].wait_recv()
        for name in ("right", "left", "twin"):
            go(bcopy[NY - d, name])
    forward(1)
    state_third(0)
    weight_step(1)
    state_last(0)
    for g in range(2):
        at = lanes(g, 0, GROUP)
        att[:, at] += dot(q[:, at], blocks[0, g], 1, 0)
    attended = att[...]
    sum_send(0, jnp.sum(attended * attended, axis=1, keepdims=True))
    for r in range(1, NY):
        bcopy[r, "right"].wait_recv()
        go(bcopy[r, "far_right"])
        go(bcopy[r, "twin_left"])
        bcopy[r, "left"].wait_recv()
        go(bcopy[r, "far_left"])
        go(bcopy[r, "twin_right"])
    inverse = 1.0 / jnp.sqrt(sum_wait(0) / MODEL + EPSILON)
    normed[pl.ds(0, TOK), :] = (att[...] * inverse).astype(BF16)

    ncopy = {
        "up": copy(normed.at[pl.ds(0, TOK)], normed.at[pl.ds(3 * TOK, TOK)], along_y(1), t),
        "down": copy(normed.at[pl.ds(0, TOK)], normed.at[pl.ds(TOK, TOK)], along_y(3), t),
        "far_up": copy(
            normed.at[pl.ds(3 * TOK, 128)], normed.at[pl.ds(2 * TOK, 128)], along_y(1), t
        ),
        "far_down": copy(
            normed.at[pl.ds(TOK + 128, 128)], normed.at[pl.ds(2 * TOK + 128, 128)], along_y(3), t
        ),
    }
    go(ncopy["up"])
    go(ncopy["down"])
    weight_step(2)
    for r in range(1, NY):
        bcopy[r, "far_right"].wait_recv()
        go(bcopy[r, "twin_far0"])
        bcopy[r, "far_left"].wait_recv()
        go(bcopy[r, "twin_far1"])
    weight_step(3)
    for name in ("twin", "twin_left", "twin_right", "twin_far0", "twin_far1"):
        for r in range(1, NY):
            bcopy[r, name].wait_recv()
    for c in own_grads:
        c.wait()

    def product(r):
        @pl.loop(0, 3)
        def _(n):
            at = pl.ds(pl.multiple_of(256 * n, 256), 256)
            part[:, at] = dot(grads[pl.ds(TOK * r, TOK), :], weights[:, at], 1, 0)

    half_up = copy(hsend.at[pl.ds(0, 128)], hrecv.at[0], along_y(1), t)
    half_down = copy(hsend.at[pl.ds(128, 128)], hrecv.at[1], along_y(3), t)
    pcopy = {}
    for i, d in enumerate((1, 3)):
        for h in (0, 1):
            at = pl.ds(128 * h, 128)
            pcopy[i, h] = copy(psend.at[i, at], precv.at[i, at], along_y(d), t)

    def chunk(off):
        j = (z + off) % NZ
        turned[...] = grads[:, pl.ds(pl.multiple_of(256 * j, 256), 256)].T

        @pl.loop(0, 3)
        def _(n):
            at = pl.ds(pl.multiple_of(256 * n, 256), 256)
            own[off, :, at] = dot(turned[...], normed[:, at], 1, 0)

    def valid(off, h):
        return own[off, pl.ds(pl.multiple_of(64 * odd + HALF * h, 32), HALF), :]

    dcopy = {}
    for step in range(4):
        for way in (0, 1):
            for h in (0, 1):
                if step > 0 or h == way:
                    at = pl.ds(HALF * h, HALF)
                    dcopy[step, way, h] = copy(
                        dsend.at[way, step, at], drecv.at[way, step, at],
                        along_z(2 * way - 1), t,
                    )

    def grad_half(step, turn):
        for way in (0, 1):
            h = way ^ (1 - turn)
            if (step, way, h) not in dcopy:
                continue
            off = 4 + step if way == 0 else 4 - step
            total = valid(off, h)
            if (step - 1, way, h) in dcopy:
                dcopy[step - 1, way, h].wait_recv()
                total = total + drecv[way, step - 1, HALF * h : HALF * (h + 1), :].astype(F32)
            dsend[way, step, HALF * h : HALF * (h + 1), :] = total.astype(BF16)
            go(dcopy[step, way, h])

    ncopy["up"].wait_recv()
    go(ncopy["far_up"])
    ncopy["down"].wait_recv()
    go(ncopy["far_down"])
    product(2)
    hsend[...] = part[...].astype(BF16)
    go(half_up)
    go(half_down)
    product(1)
    psend[0, 128:] = part[128:].astype(BF16)
    go(pcopy[0, 1])
    held[0] = part[:128]
    product(3)
    psend[1, :128] = part[:128].astype(BF16)
    go(pcopy[1, 0])
    held[1] = part[128:]
    ncopy["far_up"].wait_recv()
    ncopy["far_down"].wait_recv()
    chunk(4)
    grad_half(0, 1)

    @pl.loop(0, 2)
    def _(i):
        chunk(5 - 2 * i)

    grad_half(1, 0)
    half_up.wait_recv()
    psend[0, :128] = (held[0] + hrecv[0].astype(F32)).astype(BF16)
    go(pcopy[0, 0])
    half_down.wait_recv()
    psend[1, 128:] = (held[1] + hrecv[1].astype(F32)).astype(BF16)
    go(pcopy[1, 1])
    grad_half(1, 1)
    product(0)

    @pl.loop(0, 5)
    def _(i):
        e = i % 2
        chunk((1 - e) * ((6 + i // 2) % NZ) + e * (2 - i // 2))

    grad_half(2, 0)
    for c in pcopy.values():
        c.wait_recv()
    ng[...] = part[...] + precv[0].astype(F32) + precv[1].astype(F32)
    sum_send(1, jnp.sum(ng[...] * att[...], axis=1, keepdims=True))
    grad_half(2, 1)
    cross = sum_wait(1) * inverse
    grad_heads = (ng[...] - att[...] * (inverse * cross / MODEL)) * inverse
    gh[...] = grad_heads.astype(BF16)
    local_state(q, gh, 1)
    state_first(1)

    def backward(g):
        at = lanes(g, 0, GROUP)
        att[:, at] = dot(gh[:, at], blocks[0, g], 1, 1)
        part[:, at] = jnp.zeros((TOK, GROUP), F32)
        ng[:, at] = jnp.zeros((TOK, GROUP), F32)
        for h, (lo, hi) in enumerate(WINDOWS):
            mask = head_mask(h, lo, hi).astype(BF16)
            at = lanes(g, lo, hi)
            score = dot(gh[:, at], v[:, at] * mask, 1, 1)
            score = jnp.where(rows >= columns, score, 0.0).astype(BF16)
            att[:, at] += dot(score, k[:, at] * mask, 1, 0)
            part[:, at] += dot(score, q[:, at] * mask, 0, 0)
            ng[:, at] += dot(scores[4 * g + h], gh[:, at] * mask, 0, 0)

    backward(0)
    state_second(1)
    grad_half(3, 0)
    backward(1)
    qg[...] = att[...].astype(BF16)
    state_third(1)
    grad_half(3, 1)
    state_last(1)
    for g in range(2):
        at = lanes(g, 0, GROUP)
        kg[:, at] = (part[:, at] + dot(v[:, at], blocks[1, g], 1, 1)).astype(BF16)
        vg[:, at] = (ng[:, at] + dot(k[:, at], blocks[1, g], 1, 0)).astype(BF16)
    for h in (0, 1):
        for way in (0, 1):
            dcopy[3, way, h].wait_recv()
        at = slice(HALF * h, HALF * (h + 1))
        total = valid(0, h) + drecv[0, 3, at, :].astype(F32) + drecv[1, 3, at, :].astype(F32)
        dw[at, :] = total.astype(BF16)

    for c in started:
        c.wait_send()
    for slot in (0, 1):
        for d in range(1, NZ):
            reaches = z + d < NZ if slot == 0 else z >= d

            @pl.when(reaches)
            def _():
                states[slot][1][d - 1].wait_send()


def deliver_kernel(*refs):
    for source, target in zip(refs[:4], refs[4:]):
        target[...] = source[...]


def deliver(results):
    vmem = pl.BlockSpec(memory_space=pltpu.VMEM)
    return pl.pallas_call(
        deliver_kernel,
        out_shape=tuple(jax.ShapeDtypeStruct(x.shape, x.dtype) for x in results),
        in_specs=[vmem] * 4,
        out_specs=(vmem,) * 4,
    )(*results)


def body(q, k, v, og, w):
    vmem = pl.BlockSpec(memory_space=pltpu.VMEM)
    block = jax.ShapeDtypeStruct((TOK, COLS), BF16)
    results = pl.pallas_call(
        kernel,
        out_shape=(block, block, block, jax.ShapeDtypeStruct((CHUNK, COLS), BF16)),
        in_specs=[vmem] * 4 + [pl.BlockSpec(memory_space=pl.ANY)],
        out_specs=(vmem,) * 4,
        scratch_shapes=[
            pltpu.VMEM((NY * TOK, NZ * 256), BF16),
            pltpu.VMEM((NZ * 256, COLS), BF16),
            pltpu.VMEM((NY * TOK, COLS), BF16),
            pltpu.VMEM((8, TOK, TOK), BF16),
            pltpu.VMEM((TOK, COLS), F32),
            pltpu.VMEM((TOK, COLS), F32),
            pltpu.VMEM((TOK, COLS), F32),
            pltpu.VMEM((2, TOK, COLS), BF16),
            pltpu.VMEM((2, TOK, COLS), BF16),
            pltpu.VMEM((TOK, COLS), BF16),
            pltpu.VMEM((2, 128, COLS), BF16),
            pltpu.VMEM((2, 192, GROUP), BF16),
            pltpu.VMEM((2, NY, QUARTER, GROUP), BF16),
            pltpu.VMEM((2, QUARTER, GROUP), BF16),
            pltpu.VMEM((2, NZ, QUARTER, GROUP), BF16),
            pltpu.VMEM((QUARTER, GROUP), F32),
            pltpu.VMEM((2, NY, QUARTER, GROUP), BF16),
            pltpu.VMEM((2, 192, GROUP), BF16),
            pltpu.VMEM((2, 2, GROUP, GROUP), BF16),
            pltpu.VMEM((2, 8, TOK), F32),
            pltpu.VMEM((2, NT - 1, 8, TOK), F32),
            pltpu.VMEM((NZ, 256, COLS), F32),
            pltpu.VMEM((2, 4, CHUNK, COLS), BF16),
            pltpu.VMEM((2, 4, CHUNK, COLS), BF16),
            pltpu.VMEM((256, NY * TOK), BF16),
            pltpu.VMEM((TOK, COLS), BF16),
            pltpu.VMEM((2, 128, COLS), F32),
            pltpu.SemaphoreType.DMA((SEMS,)),
            pltpu.SemaphoreType.DMA((SEMS,)),
            pltpu.SemaphoreType.DMA((NZ,)),
        ],
        compiler_params=pltpu.CompilerParams(
            collective_id=0, has_side_effects=True, vmem_limit_bytes=56 << 20
        ),
    )(q, k, v, w.T, og)
    *grads, weight_grad = deliver(results)
    return *grads, weight_grad.T


def solution(mesh):
    placed = (P("seq", "tp"), P("seq", "tp"), P("seq", "tp"), P("seq", None), P("tp", "seq"))
    return jax.shard_map(
        body,
        mesh=mesh,
        in_specs=placed,
        out_specs=(P("seq", "tp"), P("seq", "tp"), P("seq", "tp"), P("tp", "seq")),
        check_vma=False,
    )
```

```python
import jax
import jax.numpy as jnp
from jax import lax
from jax.experimental import pallas as pl
from jax.experimental.pallas import tpu as pltpu
from jax.sharding import PartitionSpec as P

HDIM = 96
EPSILON = 1e-06
NY, NZ, NT = 4, 8, 8
TOK = 256
COLS = 768
GROUP = 384
CHUNK = 192
HALF = 96
QUARTER = 48
MODEL = 6144
WINDOWS = ((0, 128), (0, 256), (128, 384), (256, 384))
SEMS = 120
F32 = jnp.float32
BF16 = jnp.bfloat16


def dot(a, b, ca, cb):
    return lax.dot_general(a, b, (((ca,), (cb,)), ((), ())), preferred_element_type=F32)


def head_mask(h, lo, hi):
    lane = lax.broadcasted_iota(jnp.int32, (1, hi - lo), 1) + lo
    inside = (lane >= HDIM * h) & (lane < HDIM * (h + 1))
    return jnp.where(inside, 1.0, 0.0).astype(F32)


def kernel(
    q, k, v, w, og, qg, kg, vg, dw,
    grads, weights, normed, scores, att, ng, part, psend, precv, hsend, hrecv,
    lstate, lrecv, tsend, trecv, tacc, pfs, state, blocks, ssend, srecv,
    own, dsend, drecv, turned, gh, held, raw, vsend, vrecv, send, recv, lsem,
):
    s, t = lax.axis_index("seq"), lax.axis_index("tp")
    z, y = s // NY, s % NY
    core = t % 2
    odd = y % 2
    right, left, twin = (t + 2) % NT, (t + NT - 2) % NT, t + 1 - 2 * core
    count = [0]
    started = []

    def along_y(d):
        return z * NY + (y + d) % NY

    def along_z(d):
        return ((z + d + NZ) % NZ) * NY + y

    def copy(src, dst, seq, tp):
        i = count[0]
        count[0] += 1
        return pltpu.make_async_remote_copy(
            src_ref=src, dst_ref=dst, send_sem=send.at[i], recv_sem=recv.at[i],
            device_id={"seq": seq, "tp": tp}, device_id_type=pl.DeviceIdType.MESH,
        )

    def go(c):
        c.start()
        started.append(c)

    barrier = pltpu.get_barrier_semaphore()
    peers = [(along_y(d), t) for d in range(1, NY)]
    peers += [(along_z(d), t) for d in range(1, NZ)]
    peers += [(s, (t + d) % NT) for d in range(1, NT)]
    for seq, tp in peers:
        pl.semaphore_signal(
            barrier, inc=1, device_id={"seq": seq, "tp": tp}, device_id_type=pl.DeviceIdType.MESH
        )

    def window(at_z, at_y):
        return pl.multiple_of(COLS * at_z + GROUP * (at_y // 2) + 128 * (at_y % 2), 128)

    own_grads = []
    for j in range(NZ):
        c = pltpu.make_async_copy(
            og.at[:, pl.ds(window(j, y), 256)],
            grads.at[pl.ds(0, TOK), pl.ds(256 * j, 256)],
            lsem.at[j],
        )
        c.start()
        own_grads.append(c)

    for j in range(NZ):
        pad = pl.multiple_of(256 * j + CHUNK * (1 - odd), 64)
        weights[pl.ds(pad, 64), :] = jnp.zeros((64, COLS), BF16)

    def weight_rows(j, h, n):
        return pl.ds(pl.multiple_of(256 * j + 64 * odd + HALF * h, 32), n)

    weights[weight_rows(z, 0, CHUNK), :] = w[...]

    wcopy = {}
    for step in range(4):
        for way in (0, 1):
            j = (z + NZ - step) % NZ if way == 0 else (z + step) % NZ
            for h in (0, 1):
                if step < 3 or h == way:
                    rows = weight_rows(j, h, HALF)
                    wcopy[step, way, h] = copy(
                        weights.at[rows], weights.at[rows], along_z(1 - 2 * way), t
                    )
    acopy = {}
    for d in range(1, NY):
        acopy[d] = copy(
            og.at[:, pl.ds(window(t, (y + d) % NY), 256)],
            grads.at[pl.ds(TOK * (NY - d), TOK), pl.ds(pl.multiple_of(256 * t, 256), 256)],
            along_y(d), t,
        )
    bcopy = {}
    for r in range(1, NY):
        def piece(at_t, half=None):
            rows = pl.ds(TOK * r, TOK) if half is None else pl.ds(TOK * r + 128 * half, 128)
            return grads.at[rows, pl.ds(pl.multiple_of(256 * at_t, 256), 256)]

        for name, tp, at_t, half in (
            ("right", right, t, None),
            ("left", left, t, None),
            ("twin", twin, t, None),
            ("far_right", right, left, 0),
            ("far_left", left, right, 1),
            ("twin_left", twin, left, None),
            ("twin_right", twin, right, None),
            ("twin_far0", twin, (t + 4) % NT, 0),
            ("twin_far1", twin, (t + 4) % NT, 1),
        ):
            bcopy[r, name] = copy(piece(at_t, half), piece(at_t, half), s, tp)

    def weight_half(step, turn):
        for way in (0, 1):
            h = way ^ turn
            wcopy[step, way, h].wait_recv()
            if (step + 1, way, h) in wcopy:
                go(wcopy[step + 1, way, h])

    def local_state(a, b, slot):
        for g in range(2):
            full = dot(a[:, GROUP * g : GROUP * (g + 1)], b[:, GROUP * g : GROUP * (g + 1)], 0, 0)
            kept = jnp.zeros((HDIM, GROUP), F32)
            for h in range(4):
                kept = kept + full[HDIM * h : HDIM * (h + 1), :] * head_mask(h, 0, GROUP)
            lstate[slot, HDIM * g : HDIM * (g + 1), :] = kept.astype(BF16)

    states = []
    for slot in (0, 1):
        sign = 1 - 2 * slot
        first = [
            copy(
                lstate.at[slot, pl.ds(pl.multiple_of(QUARTER * ((y + d) % NY), 16), QUARTER)],
                lrecv.at[slot, y], along_y(d), t,
            )
            for d in range(1, NY)
        ]
        second = [
            copy(tsend.at[slot], trecv.at[slot, z], along_z(sign * d), t) for d in range(1, NZ)
        ]
        third = [
            copy(
                pfs.at[slot, (y + d) % NY],
                state.at[slot, pl.ds(pl.multiple_of(QUARTER * y, 16), QUARTER)],
                along_y(d), t,
            )
            for d in range(1, NY)
        ]
        states.append((first, second, third))

    def state_first(slot):
        for c in states[slot][0]:
            go(c)
        mine = pl.ds(pl.multiple_of(QUARTER * y, 16), QUARTER)
        lrecv[slot, y] = lstate[slot, mine, :]

    def state_second(slot):
        for c in states[slot][0]:
            c.wait_recv()
        total = lrecv[slot, 0].astype(F32)
        for j in range(1, NY):
            total = total + lrecv[slot, j].astype(F32)
        tsend[slot] = total.astype(BF16)
        for d in range(1, NZ):
            reaches = z + d < NZ if slot == 0 else z >= d

            @pl.when(reaches)
            def _():
                states[slot][1][d - 1].start()

    def state_third(slot):
        tacc[...] = jnp.zeros((QUARTER, GROUP), F32)
        for d in range(1, NZ):
            comes = z >= d if slot == 0 else z + d < NZ
            source = z - d if slot == 0 else z + d

            @pl.when(comes)
            def _():
                states[slot][1][d - 1].wait_recv()
                tacc[...] += trecv[slot, source].astype(F32)

        running = tacc[...]
        for j in range(NY) if slot == 0 else reversed(range(NY)):
            pfs[slot, j] = running.astype(BF16)
            running = running + lrecv[slot, j].astype(F32)
        for c in states[slot][2]:
            go(c)
        mine = pl.ds(pl.multiple_of(QUARTER * y, 16), QUARTER)
        state[slot, mine, :] = pfs[slot, y]

    def state_last(slot):
        for c in states[slot][2]:
            c.wait_recv()
        for g in range(2):
            compact = state[slot, HDIM * g : HDIM * (g + 1), :]
            for h in range(4):
                blocks[slot, g, HDIM * h : HDIM * (h + 1), :] = compact * head_mask(
                    h, 0, GROUP
                ).astype(BF16)

    sums = [
        [copy(ssend.at[i], srecv.at[i, d - 1], s, (t + d) % NT) for d in range(1, NT)]
        for i in range(2)
    ]

    def sum_send(i, column):
        ssend[i] = jnp.broadcast_to(column, (TOK, 128)).T[:8]
        for c in sums[i]:
            go(c)

    def sum_wait(i):
        total = ssend[i]
        for d in range(1, NT):
            sums[i][d - 1].wait_recv()
            total = total + srecv[i, d - 1]
        return jnp.broadcast_to(total[:1], (128, TOK)).T[:, :1]

    local_state(k, v, 0)
    pl.semaphore_wait(barrier, len(peers))
    state_first(0)
    for way in (0, 1):
        go(wcopy[0, way, way])
    for d in range(1, NY):
        go(acopy[d])

    rows = lax.broadcasted_iota(jnp.int32, (TOK, TOK), 0)
    columns = lax.broadcasted_iota(jnp.int32, (TOK, TOK), 1)

    def lanes(g, lo, hi):
        return pl.ds(pl.multiple_of(GROUP * g + lo, 128), hi - lo)

    def forward(g):
        att[:, lanes(g, 0, GROUP)] = jnp.zeros((TOK, GROUP), F32)
        for h, (lo, hi) in enumerate(WINDOWS):
            mask = head_mask(h, lo, hi).astype(BF16)
            at = lanes(g, lo, hi)
            score = dot(q[:, at], k[:, at] * mask, 1, 1)
            score = jnp.where(rows >= columns, score, 0.0).astype(BF16)
            scores[4 * g + h] = score
            att[:, at] += dot(score, v[:, at] * mask, 1, 0)

    ncopy = {
        "up": copy(raw.at[pl.ds(0, TOK)], raw.at[pl.ds(3 * TOK, TOK)], along_y(1), t),
        "down": copy(raw.at[pl.ds(0, TOK)], raw.at[pl.ds(TOK, TOK)], along_y(3), t),
        "far_up": copy(
            raw.at[pl.ds(3 * TOK, 128)], raw.at[pl.ds(2 * TOK, 128)], along_y(1), t
        ),
        "far_down": copy(
            raw.at[pl.ds(TOK + 128, 128)], raw.at[pl.ds(2 * TOK + 128, 128)], along_y(3), t
        ),
    }
    vcopy = [copy(vsend, vrecv.at[NY - d], along_y(d), t) for d in range(1, NY)]

    forward(0)
    state_second(0)
    for way in (0, 1):
        go(wcopy[0, way, 1 - way])
    weight_half(0, 0)
    for d in range(1, NY):
        acopy[d].wait_recv()
        for name in ("right", "left", "twin"):
            go(bcopy[NY - d, name])
    forward(1)
    weight_half(0, 1)
    state_third(0)
    weight_half(1, 0)
    state_last(0)
    for g in range(2):
        at = lanes(g, 0, GROUP)
        att[:, at] += dot(q[:, at], blocks[0, g], 1, 0)
    raw[pl.ds(0, TOK), :] = att[...].astype(BF16)
    go(ncopy["up"])
    go(ncopy["down"])
    sum_send(0, jnp.sum(att[...] * att[...], axis=1, keepdims=True))
    weight_half(1, 1)
    for r in range(1, NY):
        bcopy[r, "right"].wait_recv()
        go(bcopy[r, "far_right"])
        go(bcopy[r, "twin_left"])
        bcopy[r, "left"].wait_recv()
        go(bcopy[r, "far_left"])
        go(bcopy[r, "twin_right"])
    weight_half(2, 0)
    inverse = 1.0 / jnp.sqrt(sum_wait(0) / MODEL + EPSILON)
    vsend[...] = jnp.broadcast_to(inverse, (TOK, 128)).T[:8]
    for c in vcopy:
        go(c)
    weight_half(2, 1)
    ncopy["up"].wait_recv()
    go(ncopy["far_up"])
    ncopy["down"].wait_recv()
    go(ncopy["far_down"])
    for r in range(1, NY):
        bcopy[r, "far_right"].wait_recv()
        go(bcopy[r, "twin_far0"])
        bcopy[r, "far_left"].wait_recv()
        go(bcopy[r, "twin_far1"])
    weight_half(3, 0)
    for name in ("twin", "twin_left", "twin_right", "twin_far0", "twin_far1"):
        for r in range(1, NY):
            bcopy[r, name].wait_recv()
    for c in own_grads:
        c.wait()

    def product(r):
        @pl.loop(0, 3)
        def _(n):
            at = pl.ds(pl.multiple_of(256 * n, 256), 256)
            part[:, at] = dot(grads[pl.ds(TOK * r, TOK), :], weights[:, at], 1, 0)

    half_up = copy(hsend.at[pl.ds(0, 128)], hrecv.at[0], along_y(1), t)
    half_down = copy(hsend.at[pl.ds(128, 128)], hrecv.at[1], along_y(3), t)
    pcopy = {}
    for i, d in enumerate((1, 3)):
        for h in (0, 1):
            at = pl.ds(128 * h, 128)
            pcopy[i, h] = copy(psend.at[i, at], precv.at[i, at], along_y(d), t)

    def chunk(off):
        j = (z + off) % NZ
        turned[...] = grads[:, pl.ds(pl.multiple_of(256 * j, 256), 256)].T

        @pl.loop(0, 3)
        def _(n):
            at = pl.ds(pl.multiple_of(256 * n, 256), 256)
            own[off, :, at] = dot(turned[...], normed[:, at], 1, 0)

    def valid(off, h):
        return own[off, pl.ds(pl.multiple_of(64 * odd + HALF * h, 32), HALF), :]

    dcopy = {}
    for step in range(4):
        for way in (0, 1):
            for h in (0, 1):
                if step > 0 or h == way:
                    at = pl.ds(HALF * h, HALF)
                    dcopy[step, way, h] = copy(
                        dsend.at[way, step, at], drecv.at[way, step, at],
                        along_z(2 * way - 1), t,
                    )

    def grad_half(step, turn):
        for way in (0, 1):
            h = way ^ (1 - turn)
            if (step, way, h) not in dcopy:
                continue
            off = 4 + step if way == 0 else 4 - step
            total = valid(off, h)
            if (step - 1, way, h) in dcopy:
                dcopy[step - 1, way, h].wait_recv()
                total = total + drecv[way, step - 1, HALF * h : HALF * (h + 1), :].astype(F32)
            dsend[way, step, HALF * h : HALF * (h + 1), :] = total.astype(BF16)
            go(dcopy[step, way, h])

    product(2)
    hsend[...] = part[...].astype(BF16)
    go(half_up)
    go(half_down)
    ncopy["far_up"].wait_recv()
    ncopy["far_down"].wait_recv()
    for c in vcopy:
        c.wait_recv()
    for r in range(NY):
        at = pl.ds(TOK * r, TOK)
        if r == 0:
            normed[at, :] = (att[...] * inverse).astype(BF16)
        else:
            scale = jnp.broadcast_to(vrecv[r, :1], (128, TOK)).T[:, :1]
            normed[at, :] = (raw[at, :].astype(F32) * scale).astype(BF16)
    chunk(4)
    grad_half(0, 1)
    product(1)
    psend[0, 128:] = part[128:].astype(BF16)
    go(pcopy[0, 1])
    held[0] = part[:128]
    product(3)
    psend[1, :128] = part[:128].astype(BF16)
    go(pcopy[1, 0])
    held[1] = part[128:]

    @pl.loop(0, 2)
    def _(i):
        chunk(5 - 2 * i)

    grad_half(1, 0)
    half_up.wait_recv()
    psend[0, :128] = (held[0] + hrecv[0].astype(F32)).astype(BF16)
    go(pcopy[0, 0])
    half_down.wait_recv()
    psend[1, 128:] = (held[1] + hrecv[1].astype(F32)).astype(BF16)
    go(pcopy[1, 1])
    grad_half(1, 1)
    product(0)

    @pl.loop(0, 2)
    def _(i):
        chunk(6 - 4 * i)

    grad_half(2, 0)
    for c in pcopy.values():
        c.wait_recv()
    ng[...] = part[...] + precv[0].astype(F32) + precv[1].astype(F32)
    sum_send(1, jnp.sum(ng[...] * att[...], axis=1, keepdims=True))
    grad_half(2, 1)

    @pl.loop(0, 3)
    def _(i):
        chunk((1 - i + NZ) % NZ)

    cross = sum_wait(1) * inverse
    grad_heads = (ng[...] - att[...] * (inverse * cross / MODEL)) * inverse
    gh[...] = grad_heads.astype(BF16)
    local_state(q, gh, 1)
    state_first(1)

    def backward(g):
        at = lanes(g, 0, GROUP)
        att[:, at] = dot(gh[:, at], blocks[0, g], 1, 1)
        part[:, at] = jnp.zeros((TOK, GROUP), F32)
        ng[:, at] = jnp.zeros((TOK, GROUP), F32)
        for h, (lo, hi) in enumerate(WINDOWS):
            mask = head_mask(h, lo, hi).astype(BF16)
            at = lanes(g, lo, hi)
            score = dot(gh[:, at], v[:, at] * mask, 1, 1)
            score = jnp.where(rows >= columns, score, 0.0).astype(BF16)
            att[:, at] += dot(score, k[:, at] * mask, 1, 0)
            part[:, at] += dot(score, q[:, at] * mask, 0, 0)
            ng[:, at] += dot(scores[4 * g + h], gh[:, at] * mask, 0, 0)

    backward(0)
    state_second(1)
    grad_half(3, 0)
    backward(1)
    qg[...] = att[...].astype(BF16)
    state_third(1)
    grad_half(3, 1)
    state_last(1)
    for g in range(2):
        at = lanes(g, 0, GROUP)
        kg[:, at] = (part[:, at] + dot(v[:, at], blocks[1, g], 1, 1)).astype(BF16)
        vg[:, at] = (ng[:, at] + dot(k[:, at], blocks[1, g], 1, 0)).astype(BF16)
    for h in (0, 1):
        for way in (0, 1):
            dcopy[3, way, h].wait_recv()
        at = slice(HALF * h, HALF * (h + 1))
        total = valid(0, h) + drecv[0, 3, at, :].astype(F32) + drecv[1, 3, at, :].astype(F32)
        dw[at, :] = total.astype(BF16)

    for c in started:
        c.wait_send()
    for slot in (0, 1):
        for d in range(1, NZ):
            reaches = z + d < NZ if slot == 0 else z >= d

            @pl.when(reaches)
            def _():
                states[slot][1][d - 1].wait_send()


def deliver_kernel(*refs):
    for source, target in zip(refs[:4], refs[4:]):
        target[...] = source[...]


def deliver(results):
    vmem = pl.BlockSpec(memory_space=pltpu.VMEM)
    return pl.pallas_call(
        deliver_kernel,
        out_shape=tuple(jax.ShapeDtypeStruct(x.shape, x.dtype) for x in results),
        in_specs=[vmem] * 4,
        out_specs=(vmem,) * 4,
    )(*results)


def body(q, k, v, og, w):
    vmem = pl.BlockSpec(memory_space=pltpu.VMEM)
    block = jax.ShapeDtypeStruct((TOK, COLS), BF16)
    results = pl.pallas_call(
        kernel,
        out_shape=(block, block, block, jax.ShapeDtypeStruct((CHUNK, COLS), BF16)),
        in_specs=[vmem] * 4 + [pl.BlockSpec(memory_space=pl.ANY)],
        out_specs=(vmem,) * 4,
        scratch_shapes=[
            pltpu.VMEM((NY * TOK, NZ * 256), BF16),
            pltpu.VMEM((NZ * 256, COLS), BF16),
            pltpu.VMEM((NY * TOK, COLS), BF16),
            pltpu.VMEM((8, TOK, TOK), BF16),
            pltpu.VMEM((TOK, COLS), F32),
            pltpu.VMEM((TOK, COLS), F32),
            pltpu.VMEM((TOK, COLS), F32),
            pltpu.VMEM((2, TOK, COLS), BF16),
            pltpu.VMEM((2, TOK, COLS), BF16),
            pltpu.VMEM((TOK, COLS), BF16),
            pltpu.VMEM((2, 128, COLS), BF16),
            pltpu.VMEM((2, 192, GROUP), BF16),
            pltpu.VMEM((2, NY, QUARTER, GROUP), BF16),
            pltpu.VMEM((2, QUARTER, GROUP), BF16),
            pltpu.VMEM((2, NZ, QUARTER, GROUP), BF16),
            pltpu.VMEM((QUARTER, GROUP), F32),
            pltpu.VMEM((2, NY, QUARTER, GROUP), BF16),
            pltpu.VMEM((2, 192, GROUP), BF16),
            pltpu.VMEM((2, 2, GROUP, GROUP), BF16),
            pltpu.VMEM((2, 8, TOK), F32),
            pltpu.VMEM((2, NT - 1, 8, TOK), F32),
            pltpu.VMEM((NZ, 256, COLS), F32),
            pltpu.VMEM((2, 4, CHUNK, COLS), BF16),
            pltpu.VMEM((2, 4, CHUNK, COLS), BF16),
            pltpu.VMEM((256, NY * TOK), BF16),
            pltpu.VMEM((TOK, COLS), BF16),
            pltpu.VMEM((2, 128, COLS), F32),
            pltpu.VMEM((NY * TOK, COLS), BF16),
            pltpu.VMEM((8, TOK), F32),
            pltpu.VMEM((NY, 8, TOK), F32),
            pltpu.SemaphoreType.DMA((SEMS,)),
            pltpu.SemaphoreType.DMA((SEMS,)),
            pltpu.SemaphoreType.DMA((NZ,)),
        ],
        compiler_params=pltpu.CompilerParams(
            collective_id=0, has_side_effects=True, vmem_limit_bytes=56 << 20
        ),
    )(q, k, v, w.T, og)
    *grads, weight_grad = deliver(results)
    return *grads, weight_grad.T


def solution(mesh):
    placed = (P("seq", "tp"), P("seq", "tp"), P("seq", "tp"), P("seq", None), P("tp", "seq"))
    return jax.shard_map(
        body,
        mesh=mesh,
        in_specs=placed,
        out_specs=(P("seq", "tp"), P("seq", "tp"), P("seq", "tp"), P("tp", "seq")),
        check_vma=False,
    )
```

```python
import jax
import jax.numpy as jnp
from jax import lax
from jax.experimental import pallas as pl
from jax.experimental.pallas import tpu as pltpu
from jax.sharding import PartitionSpec as P

HDIM = 96
EPSILON = 1e-06
NY, NZ, NT = 4, 8, 8
TOK = 256
COLS = 768
GROUP = 384
CHUNK = 192
HALF = 96
QUARTER = 48
MODEL = 6144
WINDOWS = ((0, 128), (0, 256), (128, 384), (256, 384))
SEMS = 120
F32 = jnp.float32
BF16 = jnp.bfloat16


def dot(a, b, ca, cb):
    return lax.dot_general(a, b, (((ca,), (cb,)), ((), ())), preferred_element_type=F32)


def head_mask(h, lo, hi):
    lane = lax.broadcasted_iota(jnp.int32, (1, hi - lo), 1) + lo
    inside = (lane >= HDIM * h) & (lane < HDIM * (h + 1))
    return jnp.where(inside, 1.0, 0.0).astype(F32)


def kernel(
    q, k, v, w, og, qg, kg, vg, dw,
    grads, weights, normed, scores, att, ng, part, psend, precv, hsend, hrecv,
    lstate, lrecv, tsend, trecv, bsend, brecv, tacc, pfs, state, blocks, ssend, srecv,
    own, dsend, drecv, turned, gh, held, raw, vsend, vrecv, send, recv, lsem,
):
    s, t = lax.axis_index("seq"), lax.axis_index("tp")
    z, y = s // NY, s % NY
    core = t % 2
    odd = y % 2
    right, left, twin = (t + 2) % NT, (t + NT - 2) % NT, t + 1 - 2 * core
    count = [0]
    started = []

    def along_y(d):
        return z * NY + (y + d) % NY

    def along_z(d):
        return ((z + d + NZ) % NZ) * NY + y

    def copy(src, dst, seq, tp):
        i = count[0]
        count[0] += 1
        return pltpu.make_async_remote_copy(
            src_ref=src, dst_ref=dst, send_sem=send.at[i], recv_sem=recv.at[i],
            device_id={"seq": seq, "tp": tp}, device_id_type=pl.DeviceIdType.MESH,
        )

    def go(c):
        c.start()
        started.append(c)

    barrier = pltpu.get_barrier_semaphore()
    peers = [(along_y(d), t) for d in range(1, NY)]
    peers += [(along_z(d), t) for d in range(1, NZ)]
    peers += [(s, (t + d) % NT) for d in range(1, NT)]
    for seq, tp in peers:
        pl.semaphore_signal(
            barrier, inc=1, device_id={"seq": seq, "tp": tp}, device_id_type=pl.DeviceIdType.MESH
        )

    def window(at_z, at_y):
        return pl.multiple_of(COLS * at_z + GROUP * (at_y // 2) + 128 * (at_y % 2), 128)

    own_grads = []
    for j in range(NZ):
        c = pltpu.make_async_copy(
            og.at[:, pl.ds(window(j, y), 256)],
            grads.at[pl.ds(0, TOK), pl.ds(256 * j, 256)],
            lsem.at[j],
        )
        c.start()
        own_grads.append(c)

    for j in range(NZ):
        pad = pl.multiple_of(256 * j + CHUNK * (1 - odd), 64)
        weights[pl.ds(pad, 64), :] = jnp.zeros((64, COLS), BF16)

    def weight_rows(j, h, n):
        return pl.ds(pl.multiple_of(256 * j + 64 * odd + HALF * h, 32), n)

    weights[weight_rows(z, 0, CHUNK), :] = w[...]

    wcopy = {}
    for step in range(4):
        for way in (0, 1):
            j = (z + NZ - step) % NZ if way == 0 else (z + step) % NZ
            for h in (0, 1):
                if step < 3 or h == way:
                    rows = weight_rows(j, h, HALF)
                    wcopy[step, way, h] = copy(
                        weights.at[rows], weights.at[rows], along_z(1 - 2 * way), t
                    )
    acopy = {}
    for d in range(1, NY):
        acopy[d] = copy(
            og.at[:, pl.ds(window(t, (y + d) % NY), 256)],
            grads.at[pl.ds(TOK * (NY - d), TOK), pl.ds(pl.multiple_of(256 * t, 256), 256)],
            along_y(d), t,
        )
    bcopy = {}
    for r in range(1, NY):
        def piece(at_t, half=None):
            rows = pl.ds(TOK * r, TOK) if half is None else pl.ds(TOK * r + 128 * half, 128)
            return grads.at[rows, pl.ds(pl.multiple_of(256 * at_t, 256), 256)]

        for name, tp, at_t, half in (
            ("right", right, t, None),
            ("left", left, t, None),
            ("twin", twin, t, None),
            ("far_right", right, left, 0),
            ("far_left", left, right, 1),
            ("twin_left", twin, left, None),
            ("twin_right", twin, right, None),
            ("twin_far0", twin, (t + 4) % NT, 0),
            ("twin_far1", twin, (t + 4) % NT, 1),
        ):
            bcopy[r, name] = copy(piece(at_t, half), piece(at_t, half), s, tp)

    def weight_half(step, turn):
        for way in (0, 1):
            h = way ^ turn
            wcopy[step, way, h].wait_recv()
            if (step + 1, way, h) in wcopy:
                go(wcopy[step + 1, way, h])

    def local_state(a, b, slot):
        for g in range(2):
            full = dot(a[:, GROUP * g : GROUP * (g + 1)], b[:, GROUP * g : GROUP * (g + 1)], 0, 0)
            kept = jnp.zeros((HDIM, GROUP), F32)
            for h in range(4):
                kept = kept + full[HDIM * h : HDIM * (h + 1), :] * head_mask(h, 0, GROUP)
            lstate[slot, HDIM * g : HDIM * (g + 1), :] = kept.astype(BF16)

    place = z % 4
    outward = jnp.where(place == 3, 1, -1)
    at_edge = (place == 0) | (place == 3)
    states = []
    for slot in (0, 1):
        first = [
            copy(
                lstate.at[slot, pl.ds(pl.multiple_of(QUARTER * ((y + d) % NY), 16), QUARTER)],
                lrecv.at[slot, y], along_y(d), t,
            )
            for d in range(1, NY)
        ]
        second = [
            copy(tsend.at[slot], trecv.at[slot, place], along_z((place + d) % 4 - place), t)
            for d in range(1, 4)
        ]
        edge = [copy(bsend.at[slot], brecv.at[slot], along_z(outward * d), t) for d in (1, 2)]
        third = [
            copy(
                pfs.at[slot, (y + d) % NY],
                state.at[slot, pl.ds(pl.multiple_of(QUARTER * y, 16), QUARTER)],
                along_y(d), t,
            )
            for d in range(1, NY)
        ]
        states.append((first, second, third, edge))

    def state_first(slot):
        for c in states[slot][0]:
            go(c)
        mine = pl.ds(pl.multiple_of(QUARTER * y, 16), QUARTER)
        lrecv[slot, y] = lstate[slot, mine, :]

    def state_second(slot):
        for c in states[slot][0]:
            c.wait_recv()
        total = lrecv[slot, 0].astype(F32)
        for j in range(1, NY):
            total = total + lrecv[slot, j].astype(F32)
        tsend[slot] = total.astype(BF16)
        for c in states[slot][1]:
            go(c)
        trecv[slot, place] = tsend[slot]

    def state_middle(slot):
        for c in states[slot][1]:
            c.wait_recv()
        before, total = jnp.zeros((QUARTER, GROUP), F32), jnp.zeros((QUARTER, GROUP), F32)
        for j in range(4):
            plane = trecv[slot, j].astype(F32)
            total = total + plane
            counts = j < place if slot == 0 else j > place
            before = before + jnp.where(counts, plane, 0.0)
        tacc[...] = before
        bsend[slot] = total.astype(BF16)

        @pl.when(at_edge & (z // 4 == slot))
        def _():
            for c in states[slot][3]:
                c.start()

    def state_third(slot):
        for i, near in enumerate((at_edge, jnp.logical_not(at_edge))):

            @pl.when(near & (z // 4 == 1 - slot))
            def _():
                states[slot][3][i].wait_recv()
                tacc[...] += brecv[slot].astype(F32)

        running = tacc[...]
        for j in range(NY) if slot == 0 else reversed(range(NY)):
            pfs[slot, j] = running.astype(BF16)
            running = running + lrecv[slot, j].astype(F32)
        for c in states[slot][2]:
            go(c)
        mine = pl.ds(pl.multiple_of(QUARTER * y, 16), QUARTER)
        state[slot, mine, :] = pfs[slot, y]

    def state_last(slot):
        for c in states[slot][2]:
            c.wait_recv()
        for g in range(2):
            compact = state[slot, HDIM * g : HDIM * (g + 1), :]
            for h in range(4):
                blocks[slot, g, HDIM * h : HDIM * (h + 1), :] = compact * head_mask(
                    h, 0, GROUP
                ).astype(BF16)

    sums = [
        [copy(ssend.at[i], srecv.at[i, d - 1], s, (t + d) % NT) for d in range(1, NT)]
        for i in range(2)
    ]

    def sum_send(i, column):
        ssend[i] = jnp.broadcast_to(column, (TOK, 128)).T[:8]
        for c in sums[i]:
            go(c)

    def sum_wait(i):
        total = ssend[i]
        for d in range(1, NT):
            sums[i][d - 1].wait_recv()
            total = total + srecv[i, d - 1]
        return jnp.broadcast_to(total[:1], (128, TOK)).T[:, :1]

    local_state(k, v, 0)
    pl.semaphore_wait(barrier, len(peers))
    state_first(0)
    for way in (0, 1):
        go(wcopy[0, way, way])
    for d in range(1, NY):
        go(acopy[d])

    rows = lax.broadcasted_iota(jnp.int32, (TOK, TOK), 0)
    columns = lax.broadcasted_iota(jnp.int32, (TOK, TOK), 1)

    def lanes(g, lo, hi):
        return pl.ds(pl.multiple_of(GROUP * g + lo, 128), hi - lo)

    def forward(g):
        att[:, lanes(g, 0, GROUP)] = jnp.zeros((TOK, GROUP), F32)
        for h, (lo, hi) in enumerate(WINDOWS):
            mask = head_mask(h, lo, hi).astype(BF16)
            at = lanes(g, lo, hi)
            score = dot(q[:, at], k[:, at] * mask, 1, 1)
            score = jnp.where(rows >= columns, score, 0.0).astype(BF16)
            scores[4 * g + h] = score
            att[:, at] += dot(score, v[:, at] * mask, 1, 0)

    ncopy = {}
    for name, d, slot, first in (("up", 1, 3, 0), ("down", 3, 1, 1)):
        for turn, h in enumerate((first, 1 - first)):
            ncopy[name, turn] = copy(
                raw.at[pl.ds(128 * h, 128)], raw.at[pl.ds(TOK * slot + 128 * h, 128)],
                along_y(d), t,
            )
        ncopy[name, 2] = copy(
            raw.at[pl.ds(TOK * slot + 128 * first, 128)],
            raw.at[pl.ds(2 * TOK + 128 * first, 128)],
            along_y(d), t,
        )
    vcopy = [copy(vsend, vrecv.at[NY - d], along_y(d), t) for d in range(1, NY)]

    def turn_window(at_t):
        @pl.loop(1, NY)
        def _(r):
            block = grads[
                pl.ds(pl.multiple_of(TOK * r, TOK), TOK), pl.ds(pl.multiple_of(256 * at_t, 256), 256)
            ]
            turned[at_t, :, pl.ds(pl.multiple_of(TOK * r, TOK), TOK)] = block.T

    forward(0)
    state_second(0)
    for way in (0, 1):
        go(wcopy[0, way, 1 - way])
    state_middle(0)
    weight_half(0, 0)
    for d in range(1, NY):
        acopy[d].wait_recv()
        for name in ("right", "left", "twin"):
            go(bcopy[NY - d, name])
    forward(1)
    weight_half(0, 1)
    for c in own_grads:
        c.wait()

    @pl.loop(0, NZ)
    def _(j):
        turned[j, :, :TOK] = grads[:TOK, pl.ds(pl.multiple_of(256 * j, 256), 256)].T

    state_third(0)
    weight_half(1, 0)
    state_last(0)
    for g in range(2):
        at = lanes(g, 0, GROUP)
        att[:, at] += dot(q[:, at], blocks[0, g], 1, 0)
    raw[pl.ds(0, TOK), :] = att[...].astype(BF16)
    for turn in (0, 1):
        for name in ("up", "down"):
            go(ncopy[name, turn])
    sum_send(0, jnp.sum(att[...] * att[...], axis=1, keepdims=True))
    weight_half(1, 1)
    for r in range(1, NY):
        bcopy[r, "right"].wait_recv()
        go(bcopy[r, "far_right"])
        go(bcopy[r, "twin_left"])
        bcopy[r, "left"].wait_recv()
        go(bcopy[r, "far_left"])
        go(bcopy[r, "twin_right"])
    for at_t in (t, right, left):
        turn_window(at_t)
    weight_half(2, 0)
    for name in ("up", "down"):
        ncopy[name, 0].wait_recv()
        go(ncopy[name, 2])
    inverse = 1.0 / jnp.sqrt(sum_wait(0) / MODEL + EPSILON)
    vsend[...] = jnp.broadcast_to(inverse, (TOK, 128)).T[:8]
    for c in vcopy:
        go(c)
    weight_half(2, 1)
    for r in range(1, NY):
        bcopy[r, "far_right"].wait_recv()
        go(bcopy[r, "twin_far0"])
        bcopy[r, "far_left"].wait_recv()
        go(bcopy[r, "twin_far1"])
    for name in ("twin", "twin_left", "twin_right", "twin_far0", "twin_far1"):
        for r in range(1, NY):
            bcopy[r, name].wait_recv()
    for at_t in (twin, (twin + 2) % NT, (twin + 6) % NT, (t + 4) % NT, (twin + 4) % NT):
        turn_window(at_t)
    weight_half(3, 0)

    def product(r):
        @pl.loop(0, 3)
        def _(n):
            at = pl.ds(pl.multiple_of(256 * n, 256), 256)
            part[:, at] = dot(grads[pl.ds(TOK * r, TOK), :], weights[:, at], 1, 0)

    half_up = copy(hsend.at[pl.ds(0, 128)], hrecv.at[0], along_y(1), t)
    half_down = copy(hsend.at[pl.ds(128, 128)], hrecv.at[1], along_y(3), t)
    pcopy = {}
    for i, d in enumerate((1, 3)):
        for h in (0, 1):
            at = pl.ds(128 * h, 128)
            pcopy[i, h] = copy(psend.at[i, at], precv.at[i, at], along_y(d), t)

    def chunk(off):
        j = (z + off) % NZ

        @pl.loop(0, 3)
        def _(n):
            at = pl.ds(pl.multiple_of(256 * n, 256), 256)
            own[off, :, at] = dot(turned[j], normed[:, at], 1, 0)

    def valid(off, h):
        return own[off, pl.ds(pl.multiple_of(64 * odd + HALF * h, 32), HALF), :]

    dcopy = {}
    for step in range(4):
        for way in (0, 1):
            for h in (0, 1):
                if step > 0 or h == way:
                    at = pl.ds(HALF * h, HALF)
                    dcopy[step, way, h] = copy(
                        dsend.at[way, step, at], drecv.at[way, step, at],
                        along_z(2 * way - 1), t,
                    )

    def grad_half(step, turn):
        for way in (0, 1):
            h = way ^ (1 - turn)
            if (step, way, h) not in dcopy:
                continue
            off = 4 + step if way == 0 else 4 - step
            total = valid(off, h)
            if (step - 1, way, h) in dcopy:
                dcopy[step - 1, way, h].wait_recv()
                total = total + drecv[way, step - 1, HALF * h : HALF * (h + 1), :].astype(F32)
            dsend[way, step, HALF * h : HALF * (h + 1), :] = total.astype(BF16)
            go(dcopy[step, way, h])

    product(2)
    hsend[...] = part[...].astype(BF16)
    go(half_up)
    go(half_down)
    for name in ("up", "down"):
        ncopy[name, 1].wait_recv()
        ncopy[name, 2].wait_recv()
    for c in vcopy:
        c.wait_recv()
    for r in range(NY):
        at = pl.ds(TOK * r, TOK)
        if r == 0:
            normed[at, :] = (att[...] * inverse).astype(BF16)
        else:
            scale = jnp.broadcast_to(vrecv[r, :1], (128, TOK)).T[:, :1]
            normed[at, :] = (raw[at, :].astype(F32) * scale).astype(BF16)
    chunk(4)
    grad_half(0, 1)
    product(1)
    psend[0, 128:] = part[128:].astype(BF16)
    go(pcopy[0, 1])
    held[0] = part[:128]
    product(3)
    psend[1, :128] = part[:128].astype(BF16)
    go(pcopy[1, 0])
    held[1] = part[128:]

    @pl.loop(0, 2)
    def _(i):
        chunk(5 - 2 * i)

    grad_half(1, 0)
    half_up.wait_recv()
    psend[0, :128] = (held[0] + hrecv[0].astype(F32)).astype(BF16)
    go(pcopy[0, 0])
    half_down.wait_recv()
    psend[1, 128:] = (held[1] + hrecv[1].astype(F32)).astype(BF16)
    go(pcopy[1, 1])
    grad_half(1, 1)
    product(0)

    @pl.loop(0, 5)
    def _(i):
        e = i % 2
        chunk((1 - e) * ((6 + i // 2) % NZ) + e * (2 - i // 2))

    grad_half(2, 0)
    for c in pcopy.values():
        c.wait_recv()
    ng[...] = part[...] + precv[0].astype(F32) + precv[1].astype(F32)
    sum_send(1, jnp.sum(ng[...] * att[...], axis=1, keepdims=True))
    grad_half(2, 1)
    cross = sum_wait(1) * inverse
    grad_heads = (ng[...] - att[...] * (inverse * cross / MODEL)) * inverse
    gh[...] = grad_heads.astype(BF16)
    local_state(q, gh, 1)
    state_first(1)
    grad_half(3, 0)

    def backward(g):
        at = lanes(g, 0, GROUP)
        att[:, at] = dot(gh[:, at], blocks[0, g], 1, 1)
        part[:, at] = jnp.zeros((TOK, GROUP), F32)
        ng[:, at] = jnp.zeros((TOK, GROUP), F32)
        for h, (lo, hi) in enumerate(WINDOWS):
            mask = head_mask(h, lo, hi).astype(BF16)
            at = lanes(g, lo, hi)
            score = dot(gh[:, at], v[:, at] * mask, 1, 1)
            score = jnp.where(rows >= columns, score, 0.0).astype(BF16)
            att[:, at] += dot(score, k[:, at] * mask, 1, 0)
            part[:, at] += dot(score, q[:, at] * mask, 0, 0)
            ng[:, at] += dot(scores[4 * g + h], gh[:, at] * mask, 0, 0)

    backward(0)
    state_second(1)
    state_middle(1)
    grad_half(3, 1)
    backward(1)
    qg[...] = att[...].astype(BF16)
    state_third(1)
    state_last(1)
    for g in range(2):
        at = lanes(g, 0, GROUP)
        kg[:, at] = (part[:, at] + dot(v[:, at], blocks[1, g], 1, 1)).astype(BF16)
        vg[:, at] = (ng[:, at] + dot(k[:, at], blocks[1, g], 1, 0)).astype(BF16)
    for h in (0, 1):
        for way in (0, 1):
            dcopy[3, way, h].wait_recv()
        at = slice(HALF * h, HALF * (h + 1))
        total = valid(0, h) + drecv[0, 3, at, :].astype(F32) + drecv[1, 3, at, :].astype(F32)
        dw[at, :] = total.astype(BF16)

    for c in started:
        c.wait_send()
    for slot in (0, 1):

        @pl.when(at_edge & (z // 4 == slot))
        def _():
            for c in states[slot][3]:
                c.wait_send()


def deliver_kernel(*refs):
    for source, target in zip(refs[:4], refs[4:]):
        target[...] = source[...]


def deliver(results):
    vmem = pl.BlockSpec(memory_space=pltpu.VMEM)
    return pl.pallas_call(
        deliver_kernel,
        out_shape=tuple(jax.ShapeDtypeStruct(x.shape, x.dtype) for x in results),
        in_specs=[vmem] * 4,
        out_specs=(vmem,) * 4,
    )(*results)


def body(q, k, v, og, w):
    vmem = pl.BlockSpec(memory_space=pltpu.VMEM)
    block = jax.ShapeDtypeStruct((TOK, COLS), BF16)
    results = pl.pallas_call(
        kernel,
        out_shape=(block, block, block, jax.ShapeDtypeStruct((CHUNK, COLS), BF16)),
        in_specs=[vmem] * 4 + [pl.BlockSpec(memory_space=pl.ANY)],
        out_specs=(vmem,) * 4,
        scratch_shapes=[
            pltpu.VMEM((NY * TOK, NZ * 256), BF16),
            pltpu.VMEM((NZ * 256, COLS), BF16),
            pltpu.VMEM((NY * TOK, COLS), BF16),
            pltpu.VMEM((8, TOK, TOK), BF16),
            pltpu.VMEM((TOK, COLS), F32),
            pltpu.VMEM((TOK, COLS), F32),
            pltpu.VMEM((TOK, COLS), F32),
            pltpu.VMEM((2, TOK, COLS), BF16),
            pltpu.VMEM((2, TOK, COLS), BF16),
            pltpu.VMEM((TOK, COLS), BF16),
            pltpu.VMEM((2, 128, COLS), BF16),
            pltpu.VMEM((2, 192, GROUP), BF16),
            pltpu.VMEM((2, NY, QUARTER, GROUP), BF16),
            pltpu.VMEM((2, QUARTER, GROUP), BF16),
            pltpu.VMEM((2, 4, QUARTER, GROUP), BF16),
            pltpu.VMEM((2, QUARTER, GROUP), BF16),
            pltpu.VMEM((2, QUARTER, GROUP), BF16),
            pltpu.VMEM((QUARTER, GROUP), F32),
            pltpu.VMEM((2, NY, QUARTER, GROUP), BF16),
            pltpu.VMEM((2, 192, GROUP), BF16),
            pltpu.VMEM((2, 2, GROUP, GROUP), BF16),
            pltpu.VMEM((2, 8, TOK), F32),
            pltpu.VMEM((2, NT - 1, 8, TOK), F32),
            pltpu.VMEM((NZ, 256, COLS), F32),
            pltpu.VMEM((2, 4, CHUNK, COLS), BF16),
            pltpu.VMEM((2, 4, CHUNK, COLS), BF16),
            pltpu.VMEM((NZ, 256, NY * TOK), BF16),
            pltpu.VMEM((TOK, COLS), BF16),
            pltpu.VMEM((2, 128, COLS), F32),
            pltpu.VMEM((NY * TOK, COLS), BF16),
            pltpu.VMEM((8, TOK), F32),
            pltpu.VMEM((NY, 8, TOK), F32),
            pltpu.SemaphoreType.DMA((SEMS,)),
            pltpu.SemaphoreType.DMA((SEMS,)),
            pltpu.SemaphoreType.DMA((NZ,)),
        ],
        compiler_params=pltpu.CompilerParams(
            collective_id=0, has_side_effects=True, vmem_limit_bytes=56 << 20
        ),
    )(q, k, v, w.T, og)
    *grads, weight_grad = deliver(results)
    return *grads, weight_grad.T


def solution(mesh):
    placed = (P("seq", "tp"), P("seq", "tp"), P("seq", "tp"), P("seq", None), P("tp", "seq"))
    return jax.shard_map(
        body,
        mesh=mesh,
        in_specs=placed,
        out_specs=(P("seq", "tp"), P("seq", "tp"), P("seq", "tp"), P("tp", "seq")),
        check_vma=False,
    )
```

```python
import jax
import jax.numpy as jnp
from jax import lax
from jax.experimental import pallas as pl
from jax.experimental.pallas import tpu as pltpu
from jax.sharding import PartitionSpec as P

HDIM = 96
EPSILON = 1e-06
NY, NZ, NT = 4, 8, 8
TOK = 256
COLS = 768
GROUP = 384
CHUNK = 192
HALF = 96
QUARTER = 48
MODEL = 6144
WINDOWS = ((0, 128), (0, 256), (128, 384), (256, 384))
SEMS = 120
F32 = jnp.float32
BF16 = jnp.bfloat16


def dot(a, b, ca, cb):
    return lax.dot_general(a, b, (((ca,), (cb,)), ((), ())), preferred_element_type=F32)


def head_mask(h, lo, hi):
    lane = lax.broadcasted_iota(jnp.int32, (1, hi - lo), 1) + lo
    inside = (lane >= HDIM * h) & (lane < HDIM * (h + 1))
    return jnp.where(inside, 1.0, 0.0).astype(F32)


def kernel(
    q_in, k_in, v_in, w_in, og, qg, kg, vg, dw,
    q, k, v,
    grads, weights, normed, scores, att, ng, part, psend, precv, hsend, hrecv,
    lstate, lrecv, tsend, trecv, bsend, brecv, tacc, pfs, state, blocks, ssend, srecv,
    own, dsend, drecv, turned, gh, held, raw, vsend, vrecv, send, recv, lsem,
):
    s, t = lax.axis_index("seq"), lax.axis_index("tp")
    z, y = s // NY, s % NY
    core = t % 2
    odd = y % 2
    right, left, twin = (t + 2) % NT, (t + NT - 2) % NT, t + 1 - 2 * core
    count = [0]
    started = []

    def along_y(d):
        return z * NY + (y + d) % NY

    def along_z(d):
        return ((z + d + NZ) % NZ) * NY + y

    def copy(src, dst, seq, tp):
        i = count[0]
        count[0] += 1
        return pltpu.make_async_remote_copy(
            src_ref=src, dst_ref=dst, send_sem=send.at[i], recv_sem=recv.at[i],
            device_id={"seq": seq, "tp": tp}, device_id_type=pl.DeviceIdType.MESH,
        )

    def go(c):
        c.start()
        started.append(c)

    barrier = pltpu.get_barrier_semaphore()
    peers = [(along_y(d), t) for d in range(1, NY)]
    peers += [(along_z(d), t) for d in range(1, NZ)]
    peers += [(s, (t + d) % NT) for d in range(1, NT)]
    for seq, tp in peers:
        pl.semaphore_signal(
            barrier, inc=1, device_id={"seq": seq, "tp": tp}, device_id_type=pl.DeviceIdType.MESH
        )

    def window(at_z, at_y):
        return pl.multiple_of(COLS * at_z + GROUP * (at_y // 2) + 128 * (at_y % 2), 128)

    def weight_rows(j, h, n):
        return pl.ds(pl.multiple_of(256 * j + 64 * odd + HALF * h, 32), n)

    loads = [
        pltpu.make_async_copy(source, target, lsem.at[NZ + i])
        for i, (source, target) in enumerate(
            ((w_in, weights.at[weight_rows(z, 0, CHUNK)]), (k_in, k), (v_in, v), (q_in, q))
        )
    ]
    for c in loads:
        c.start()
    own_grads = []
    for j in range(NZ):
        c = pltpu.make_async_copy(
            og.at[:, pl.ds(window(j, y), 256)],
            grads.at[pl.ds(0, TOK), pl.ds(256 * j, 256)],
            lsem.at[j],
        )
        c.start()
        own_grads.append(c)

    for j in range(NZ):
        pad = pl.multiple_of(256 * j + CHUNK * (1 - odd), 64)
        weights[pl.ds(pad, 64), :] = jnp.zeros((64, COLS), BF16)

    wcopy = {}
    for step in range(4):
        for way in (0, 1):
            j = (z + NZ - step) % NZ if way == 0 else (z + step) % NZ
            for h in (0, 1):
                if step < 3 or h == way:
                    rows = weight_rows(j, h, HALF)
                    wcopy[step, way, h] = copy(
                        weights.at[rows], weights.at[rows], along_z(1 - 2 * way), t
                    )
    acopy = {}
    for d in range(1, NY):
        acopy[d] = copy(
            og.at[:, pl.ds(window(t, (y + d) % NY), 256)],
            grads.at[pl.ds(TOK * (NY - d), TOK), pl.ds(pl.multiple_of(256 * t, 256), 256)],
            along_y(d), t,
        )
    bcopy = {}
    for r in range(1, NY):
        def piece(at_t, half=None):
            rows = pl.ds(TOK * r, TOK) if half is None else pl.ds(TOK * r + 128 * half, 128)
            return grads.at[rows, pl.ds(pl.multiple_of(256 * at_t, 256), 256)]

        for name, tp, at_t, half in (
            ("right", right, t, None),
            ("left", left, t, None),
            ("twin", twin, t, None),
            ("far_right", right, left, 0),
            ("far_left", left, right, 1),
            ("twin_left", twin, left, None),
            ("twin_right", twin, right, None),
            ("twin_far0", twin, (t + 4) % NT, 0),
            ("twin_far1", twin, (t + 4) % NT, 1),
        ):
            bcopy[r, name] = copy(piece(at_t, half), piece(at_t, half), s, tp)

    def weight_half(step, turn):
        for way in (0, 1):
            h = way ^ turn
            wcopy[step, way, h].wait_recv()
            if (step + 1, way, h) in wcopy:
                go(wcopy[step + 1, way, h])

    def local_state(a, b, slot):
        for g in range(2):
            full = dot(a[:, GROUP * g : GROUP * (g + 1)], b[:, GROUP * g : GROUP * (g + 1)], 0, 0)
            kept = jnp.zeros((HDIM, GROUP), F32)
            for h in range(4):
                kept = kept + full[HDIM * h : HDIM * (h + 1), :] * head_mask(h, 0, GROUP)
            lstate[slot, HDIM * g : HDIM * (g + 1), :] = kept.astype(BF16)

    place = z % 4
    outward = jnp.where(place == 3, 1, -1)
    at_edge = (place == 0) | (place == 3)
    states = []
    for slot in (0, 1):
        first = [
            copy(
                lstate.at[slot, pl.ds(pl.multiple_of(QUARTER * ((y + d) % NY), 16), QUARTER)],
                lrecv.at[slot, y], along_y(d), t,
            )
            for d in range(1, NY)
        ]
        second = [
            copy(tsend.at[slot], trecv.at[slot, place], along_z((place + d) % 4 - place), t)
            for d in range(1, 4)
        ]
        edge = [copy(bsend.at[slot], brecv.at[slot], along_z(outward * d), t) for d in (1, 2)]
        third = [
            copy(
                pfs.at[slot, (y + d) % NY],
                state.at[slot, pl.ds(pl.multiple_of(QUARTER * y, 16), QUARTER)],
                along_y(d), t,
            )
            for d in range(1, NY)
        ]
        states.append((first, second, third, edge))

    def state_first(slot):
        for c in states[slot][0]:
            go(c)
        mine = pl.ds(pl.multiple_of(QUARTER * y, 16), QUARTER)
        lrecv[slot, y] = lstate[slot, mine, :]

    def state_second(slot):
        for c in states[slot][0]:
            c.wait_recv()
        total = lrecv[slot, 0].astype(F32)
        for j in range(1, NY):
            total = total + lrecv[slot, j].astype(F32)
        tsend[slot] = total.astype(BF16)
        for c in states[slot][1]:
            go(c)
        trecv[slot, place] = tsend[slot]

    def state_middle(slot):
        for c in states[slot][1]:
            c.wait_recv()
        before, total = jnp.zeros((QUARTER, GROUP), F32), jnp.zeros((QUARTER, GROUP), F32)
        for j in range(4):
            plane = trecv[slot, j].astype(F32)
            total = total + plane
            counts = j < place if slot == 0 else j > place
            before = before + jnp.where(counts, plane, 0.0)
        tacc[...] = before
        bsend[slot] = total.astype(BF16)

        @pl.when(at_edge & (z // 4 == slot))
        def _():
            for c in states[slot][3]:
                c.start()

    def state_third(slot):
        for i, near in enumerate((at_edge, jnp.logical_not(at_edge))):

            @pl.when(near & (z // 4 == 1 - slot))
            def _():
                states[slot][3][i].wait_recv()
                tacc[...] += brecv[slot].astype(F32)

        running = tacc[...]
        for j in range(NY) if slot == 0 else reversed(range(NY)):
            pfs[slot, j] = running.astype(BF16)
            running = running + lrecv[slot, j].astype(F32)
        for c in states[slot][2]:
            go(c)
        mine = pl.ds(pl.multiple_of(QUARTER * y, 16), QUARTER)
        state[slot, mine, :] = pfs[slot, y]

    def state_last(slot):
        for c in states[slot][2]:
            c.wait_recv()
        for g in range(2):
            compact = state[slot, HDIM * g : HDIM * (g + 1), :]
            for h in range(4):
                blocks[slot, g, HDIM * h : HDIM * (h + 1), :] = compact * head_mask(
                    h, 0, GROUP
                ).astype(BF16)

    sums = [
        [copy(ssend.at[i], srecv.at[i, d - 1], s, (t + d) % NT) for d in range(1, NT)]
        for i in range(2)
    ]

    def sum_send(i, column):
        ssend[i] = jnp.broadcast_to(column, (TOK, 128)).T[:8]
        for c in sums[i]:
            go(c)

    def sum_wait(i):
        total = ssend[i]
        for d in range(1, NT):
            sums[i][d - 1].wait_recv()
            total = total + srecv[i, d - 1]
        return jnp.broadcast_to(total[:1], (128, TOK)).T[:, :1]

    for c in loads:
        c.wait()
    local_state(k, v, 0)
    pl.semaphore_wait(barrier, len(peers))
    state_first(0)
    for way in (0, 1):
        go(wcopy[0, way, way])
    for d in range(1, NY):
        go(acopy[d])

    rows = lax.broadcasted_iota(jnp.int32, (TOK, TOK), 0)
    columns = lax.broadcasted_iota(jnp.int32, (TOK, TOK), 1)

    def lanes(g, lo, hi):
        return pl.ds(pl.multiple_of(GROUP * g + lo, 128), hi - lo)

    def forward(g):
        att[:, lanes(g, 0, GROUP)] = jnp.zeros((TOK, GROUP), F32)
        for h, (lo, hi) in enumerate(WINDOWS):
            mask = head_mask(h, lo, hi).astype(BF16)
            at = lanes(g, lo, hi)
            score = dot(q[:, at], k[:, at] * mask, 1, 1)
            score = jnp.where(rows >= columns, score, 0.0).astype(BF16)
            scores[4 * g + h] = score
            att[:, at] += dot(score, v[:, at] * mask, 1, 0)

    ncopy = {}
    for name, d, slot, first in (("up", 1, 3, 0), ("down", 3, 1, 1)):
        for turn, h in enumerate((first, 1 - first)):
            ncopy[name, turn] = copy(
                raw.at[pl.ds(128 * h, 128)], raw.at[pl.ds(TOK * slot + 128 * h, 128)],
                along_y(d), t,
            )
        ncopy[name, 2] = copy(
            raw.at[pl.ds(TOK * slot + 128 * first, 128)],
            raw.at[pl.ds(2 * TOK + 128 * first, 128)],
            along_y(d), t,
        )
    vcopy = [copy(vsend, vrecv.at[NY - d], along_y(d), t) for d in range(1, NY)]

    def turn_window(at_t):
        @pl.loop(1, NY)
        def _(r):
            block = grads[
                pl.ds(pl.multiple_of(TOK * r, TOK), TOK), pl.ds(pl.multiple_of(256 * at_t, 256), 256)
            ]
            turned[at_t, :, pl.ds(pl.multiple_of(TOK * r, TOK), TOK)] = block.T

    forward(0)
    state_second(0)
    for way in (0, 1):
        go(wcopy[0, way, 1 - way])
    state_middle(0)
    weight_half(0, 0)
    for d in range(1, NY):
        acopy[d].wait_recv()
        for name in ("right", "left", "twin"):
            go(bcopy[NY - d, name])
    forward(1)
    weight_half(0, 1)
    for c in own_grads:
        c.wait()

    @pl.loop(0, NZ)
    def _(j):
        turned[j, :, :TOK] = grads[:TOK, pl.ds(pl.multiple_of(256 * j, 256), 256)].T

    state_third(0)
    weight_half(1, 0)
    state_last(0)
    for g in range(2):
        at = lanes(g, 0, GROUP)
        att[:, at] += dot(q[:, at], blocks[0, g], 1, 0)
    raw[pl.ds(0, TOK), :] = att[...].astype(BF16)
    for turn in (0, 1):
        for name in ("up", "down"):
            go(ncopy[name, turn])
    sum_send(0, jnp.sum(att[...] * att[...], axis=1, keepdims=True))
    weight_half(1, 1)
    for r in range(1, NY):
        bcopy[r, "right"].wait_recv()
        go(bcopy[r, "far_right"])
        go(bcopy[r, "twin_left"])
        bcopy[r, "left"].wait_recv()
        go(bcopy[r, "far_left"])
        go(bcopy[r, "twin_right"])
    for at_t in (t, right, left):
        turn_window(at_t)
    weight_half(2, 0)
    for name in ("up", "down"):
        ncopy[name, 0].wait_recv()
        go(ncopy[name, 2])
    inverse = 1.0 / jnp.sqrt(sum_wait(0) / MODEL + EPSILON)
    vsend[...] = jnp.broadcast_to(inverse, (TOK, 128)).T[:8]
    for c in vcopy:
        go(c)
    weight_half(2, 1)
    for r in range(1, NY):
        bcopy[r, "far_right"].wait_recv()
        go(bcopy[r, "twin_far0"])
        bcopy[r, "far_left"].wait_recv()
        go(bcopy[r, "twin_far1"])
    for name in ("twin", "twin_left", "twin_right", "twin_far0", "twin_far1"):
        for r in range(1, NY):
            bcopy[r, name].wait_recv()
    for at_t in (twin, (twin + 2) % NT, (twin + 6) % NT, (t + 4) % NT, (twin + 4) % NT):
        turn_window(at_t)
    weight_half(3, 0)

    def product(r):
        @pl.loop(0, 3)
        def _(n):
            at = pl.ds(pl.multiple_of(256 * n, 256), 256)
            part[:, at] = dot(grads[pl.ds(TOK * r, TOK), :], weights[:, at], 1, 0)

    half_up = copy(hsend.at[pl.ds(0, 128)], hrecv.at[0], along_y(1), t)
    half_down = copy(hsend.at[pl.ds(128, 128)], hrecv.at[1], along_y(3), t)
    pcopy = {}
    for i, d in enumerate((1, 3)):
        for h in (0, 1):
            at = pl.ds(128 * h, 128)
            pcopy[i, h] = copy(psend.at[i, at], precv.at[i, at], along_y(d), t)

    def chunk(off):
        j = (z + off) % NZ

        @pl.loop(0, 3)
        def _(n):
            at = pl.ds(pl.multiple_of(256 * n, 256), 256)
            own[off, :, at] = dot(turned[j], normed[:, at], 1, 0)

    def valid(off, h):
        return own[off, pl.ds(pl.multiple_of(64 * odd + HALF * h, 32), HALF), :]

    dcopy = {}
    for step in range(4):
        for way in (0, 1):
            for h in (0, 1):
                if step > 0 or h == way:
                    at = pl.ds(HALF * h, HALF)
                    dcopy[step, way, h] = copy(
                        dsend.at[way, step, at], drecv.at[way, step, at],
                        along_z(2 * way - 1), t,
                    )

    def grad_half(step, turn):
        for way in (0, 1):
            h = way ^ (1 - turn)
            if (step, way, h) not in dcopy:
                continue
            off = 4 + step if way == 0 else 4 - step
            total = valid(off, h)
            if (step - 1, way, h) in dcopy:
                dcopy[step - 1, way, h].wait_recv()
                total = total + drecv[way, step - 1, HALF * h : HALF * (h + 1), :].astype(F32)
            dsend[way, step, HALF * h : HALF * (h + 1), :] = total.astype(BF16)
            go(dcopy[step, way, h])

    product(2)
    hsend[...] = part[...].astype(BF16)
    go(half_up)
    go(half_down)
    for name in ("up", "down"):
        ncopy[name, 1].wait_recv()
        ncopy[name, 2].wait_recv()
    for c in vcopy:
        c.wait_recv()
    for r in range(NY):
        at = pl.ds(TOK * r, TOK)
        if r == 0:
            normed[at, :] = (att[...] * inverse).astype(BF16)
        else:
            scale = jnp.broadcast_to(vrecv[r, :1], (128, TOK)).T[:, :1]
            normed[at, :] = (raw[at, :].astype(F32) * scale).astype(BF16)
    chunk(4)
    grad_half(0, 1)
    product(1)
    psend[0, 128:] = part[128:].astype(BF16)
    go(pcopy[0, 1])
    held[0] = part[:128]
    product(3)
    psend[1, :128] = part[:128].astype(BF16)
    go(pcopy[1, 0])
    held[1] = part[128:]

    @pl.loop(0, 2)
    def _(i):
        chunk(5 - 2 * i)

    grad_half(1, 0)
    half_up.wait_recv()
    psend[0, :128] = (held[0] + hrecv[0].astype(F32)).astype(BF16)
    go(pcopy[0, 0])
    half_down.wait_recv()
    psend[1, 128:] = (held[1] + hrecv[1].astype(F32)).astype(BF16)
    go(pcopy[1, 1])
    grad_half(1, 1)
    product(0)

    @pl.loop(0, 5)
    def _(i):
        e = i % 2
        chunk((1 - e) * ((6 + i // 2) % NZ) + e * (2 - i // 2))

    grad_half(2, 0)
    for c in pcopy.values():
        c.wait_recv()
    ng[...] = part[...] + precv[0].astype(F32) + precv[1].astype(F32)
    sum_send(1, jnp.sum(ng[...] * att[...], axis=1, keepdims=True))
    grad_half(2, 1)
    cross = sum_wait(1) * inverse
    grad_heads = (ng[...] - att[...] * (inverse * cross / MODEL)) * inverse
    gh[...] = grad_heads.astype(BF16)
    local_state(q, gh, 1)
    state_first(1)
    grad_half(3, 0)

    def backward(g):
        at = lanes(g, 0, GROUP)
        att[:, at] = dot(gh[:, at], blocks[0, g], 1, 1)
        part[:, at] = jnp.zeros((TOK, GROUP), F32)
        ng[:, at] = jnp.zeros((TOK, GROUP), F32)
        for h, (lo, hi) in enumerate(WINDOWS):
            mask = head_mask(h, lo, hi).astype(BF16)
            at = lanes(g, lo, hi)
            score = dot(gh[:, at], v[:, at] * mask, 1, 1)
            score = jnp.where(rows >= columns, score, 0.0).astype(BF16)
            att[:, at] += dot(score, k[:, at] * mask, 1, 0)
            part[:, at] += dot(score, q[:, at] * mask, 0, 0)
            ng[:, at] += dot(scores[4 * g + h], gh[:, at] * mask, 0, 0)

    backward(0)
    state_second(1)
    state_middle(1)
    grad_half(3, 1)
    backward(1)
    qg[...] = att[...].astype(BF16)
    state_third(1)
    state_last(1)
    for g in range(2):
        at = lanes(g, 0, GROUP)
        kg[:, at] = (part[:, at] + dot(v[:, at], blocks[1, g], 1, 1)).astype(BF16)
        vg[:, at] = (ng[:, at] + dot(k[:, at], blocks[1, g], 1, 0)).astype(BF16)
    for h in (0, 1):
        for way in (0, 1):
            dcopy[3, way, h].wait_recv()
        at = slice(HALF * h, HALF * (h + 1))
        total = valid(0, h) + drecv[0, 3, at, :].astype(F32) + drecv[1, 3, at, :].astype(F32)
        dw[at, :] = total.astype(BF16)

    for c in started:
        c.wait_send()
    for slot in (0, 1):

        @pl.when(at_edge & (z // 4 == slot))
        def _():
            for c in states[slot][3]:
                c.wait_send()


def deliver_kernel(*refs):
    sems = refs[-1]
    copies = [pltpu.make_async_copy(refs[i], refs[4 + i], sems.at[i]) for i in range(4)]
    for c in copies:
        c.start()
    for c in copies:
        c.wait()


def deliver(results):
    vmem = pl.BlockSpec(memory_space=pltpu.VMEM)
    return pl.pallas_call(
        deliver_kernel,
        out_shape=tuple(jax.ShapeDtypeStruct(x.shape, x.dtype) for x in results),
        in_specs=[vmem] * 4,
        out_specs=(pl.BlockSpec(memory_space=pl.ANY),) * 4,
        scratch_shapes=[pltpu.SemaphoreType.DMA((4,))],
    )(*results)


def body(q, k, v, og, w):
    vmem = pl.BlockSpec(memory_space=pltpu.VMEM)
    block = pltpu.VMEM((TOK, COLS), BF16)
    results = pl.pallas_call(
        kernel,
        out_shape=(block, block, block, pltpu.VMEM((CHUNK, COLS), BF16)),
        in_specs=[pl.BlockSpec(memory_space=pltpu.HBM)] * 5,
        out_specs=(vmem,) * 4,
        scratch_shapes=[
            pltpu.VMEM((TOK, COLS), BF16),
            pltpu.VMEM((TOK, COLS), BF16),
            pltpu.VMEM((TOK, COLS), BF16),
            pltpu.VMEM((NY * TOK, NZ * 256), BF16),
            pltpu.VMEM((NZ * 256, COLS), BF16),
            pltpu.VMEM((NY * TOK, COLS), BF16),
            pltpu.VMEM((8, TOK, TOK), BF16),
            pltpu.VMEM((TOK, COLS), F32),
            pltpu.VMEM((TOK, COLS), F32),
            pltpu.VMEM((TOK, COLS), F32),
            pltpu.VMEM((2, TOK, COLS), BF16),
            pltpu.VMEM((2, TOK, COLS), BF16),
            pltpu.VMEM((TOK, COLS), BF16),
            pltpu.VMEM((2, 128, COLS), BF16),
            pltpu.VMEM((2, 192, GROUP), BF16),
            pltpu.VMEM((2, NY, QUARTER, GROUP), BF16),
            pltpu.VMEM((2, QUARTER, GROUP), BF16),
            pltpu.VMEM((2, 4, QUARTER, GROUP), BF16),
            pltpu.VMEM((2, QUARTER, GROUP), BF16),
            pltpu.VMEM((2, QUARTER, GROUP), BF16),
            pltpu.VMEM((QUARTER, GROUP), F32),
            pltpu.VMEM((2, NY, QUARTER, GROUP), BF16),
            pltpu.VMEM((2, 192, GROUP), BF16),
            pltpu.VMEM((2, 2, GROUP, GROUP), BF16),
            pltpu.VMEM((2, 8, TOK), F32),
            pltpu.VMEM((2, NT - 1, 8, TOK), F32),
            pltpu.VMEM((NZ, 256, COLS), F32),
            pltpu.VMEM((2, 4, CHUNK, COLS), BF16),
            pltpu.VMEM((2, 4, CHUNK, COLS), BF16),
            pltpu.VMEM((NZ, 256, NY * TOK), BF16),
            pltpu.VMEM((TOK, COLS), BF16),
            pltpu.VMEM((2, 128, COLS), F32),
            pltpu.VMEM((NY * TOK, COLS), BF16),
            pltpu.VMEM((8, TOK), F32),
            pltpu.VMEM((NY, 8, TOK), F32),
            pltpu.SemaphoreType.DMA((SEMS,)),
            pltpu.SemaphoreType.DMA((SEMS,)),
            pltpu.SemaphoreType.DMA((NZ + 4,)),
        ],
        compiler_params=pltpu.CompilerParams(
            collective_id=0, has_side_effects=True, vmem_limit_bytes=56 << 20
        ),
    )(q, k, v, w.T, og)
    *grads, weight_grad = deliver([pltpu.with_memory_space_constraint(x, pltpu.VMEM) for x in results])
    return *grads, weight_grad.T


def solution(mesh):
    placed = (P("seq", "tp"), P("seq", "tp"), P("seq", "tp"), P("seq", None), P("tp", "seq"))
    return jax.shard_map(
        body,
        mesh=mesh,
        in_specs=placed,
        out_specs=(P("seq", "tp"), P("seq", "tp"), P("seq", "tp"), P("tp", "seq")),
        check_vma=False,
    )
```

```python
import jax
import jax.numpy as jnp
from jax import lax
from jax.experimental import pallas as pl
from jax.experimental.pallas import tpu as pltpu
from jax.sharding import PartitionSpec as P

HDIM = 96
EPSILON = 1e-06
NY, NZ, NT = 4, 8, 8
TOK = 256
COLS = 768
GROUP = 384
CHUNK = 192
HALF = 96
QUARTER = 48
MODEL = 6144
WINDOWS = ((0, 128), (0, 256), (128, 384), (256, 384))
SEMS = 120
F32 = jnp.float32
BF16 = jnp.bfloat16


def dot(a, b, ca, cb):
    return lax.dot_general(a, b, (((ca,), (cb,)), ((), ())), preferred_element_type=F32)


def head_mask(h, lo, hi):
    lane = lax.broadcasted_iota(jnp.int32, (1, hi - lo), 1) + lo
    inside = (lane >= HDIM * h) & (lane < HDIM * (h + 1))
    return jnp.where(inside, 1.0, 0.0).astype(F32)


def kernel(
    q_in, k_in, v_in, w_in, og, qg, kg, vg, dw,
    q, k, v,
    grads, weights, normed, scores, att, ng, part, psend, precv, hsend, hrecv,
    lstate, lrecv, tsend, trecv, bsend, brecv, tacc, pfs, state, blocks, ssend, srecv,
    own, dsend, drecv, turned, gh, held, raw, vsend, vrecv, send, recv, lsem,
):
    s, t = lax.axis_index("seq"), lax.axis_index("tp")
    z, y = s // NY, s % NY
    core = t % 2
    odd = y % 2
    right, left, twin = (t + 2) % NT, (t + NT - 2) % NT, t + 1 - 2 * core
    count = [0]
    started = []

    def along_y(d):
        return z * NY + (y + d) % NY

    def along_z(d):
        return ((z + d + NZ) % NZ) * NY + y

    def copy(src, dst, seq, tp):
        i = count[0]
        count[0] += 1
        return pltpu.make_async_remote_copy(
            src_ref=src, dst_ref=dst, send_sem=send.at[i], recv_sem=recv.at[i],
            device_id={"seq": seq, "tp": tp}, device_id_type=pl.DeviceIdType.MESH,
        )

    def go(c):
        c.start()
        started.append(c)

    barrier = pltpu.get_barrier_semaphore()
    peers = [(along_y(d), t) for d in range(1, NY)]
    peers += [(along_z(d), t) for d in range(1, NZ)]
    peers += [(s, (t + d) % NT) for d in range(1, NT)]
    for seq, tp in peers:
        pl.semaphore_signal(
            barrier, inc=1, device_id={"seq": seq, "tp": tp}, device_id_type=pl.DeviceIdType.MESH
        )

    def window(at_z, at_y):
        return pl.multiple_of(COLS * at_z + GROUP * (at_y // 2) + 128 * (at_y % 2), 128)

    def weight_rows(j, h, n):
        return pl.ds(pl.multiple_of(256 * j + 64 * odd + HALF * h, 32), n)

    loads = [
        pltpu.make_async_copy(source, target, lsem.at[NZ + i])
        for i, (source, target) in enumerate(
            ((w_in, weights.at[weight_rows(z, 0, CHUNK)]), (k_in, k), (v_in, v), (q_in, q))
        )
    ]
    for c in loads:
        c.start()
    own_grads = []
    for j in range(NZ):
        c = pltpu.make_async_copy(
            og.at[:, pl.ds(window(j, y), 256)],
            grads.at[pl.ds(0, TOK), pl.ds(256 * j, 256)],
            lsem.at[j],
        )
        c.start()
        own_grads.append(c)

    for j in range(NZ):
        pad = pl.multiple_of(256 * j + CHUNK * (1 - odd), 64)
        weights[pl.ds(pad, 64), :] = jnp.zeros((64, COLS), BF16)

    wcopy = {}
    for step in range(4):
        for way in (0, 1):
            j = (z + NZ - step) % NZ if way == 0 else (z + step) % NZ
            for h in (0, 1):
                if step < 3 or h == way:
                    rows = weight_rows(j, h, HALF)
                    wcopy[step, way, h] = copy(
                        weights.at[rows], weights.at[rows], along_z(1 - 2 * way), t
                    )
    acopy = {}
    for d in range(1, NY):
        acopy[d] = copy(
            og.at[:, pl.ds(window(t, (y + d) % NY), 256)],
            grads.at[pl.ds(TOK * (NY - d), TOK), pl.ds(pl.multiple_of(256 * t, 256), 256)],
            along_y(d), t,
        )
    bcopy = {}
    for r in range(1, NY):
        def piece(at_t, half=None):
            rows = pl.ds(TOK * r, TOK) if half is None else pl.ds(TOK * r + 128 * half, 128)
            return grads.at[rows, pl.ds(pl.multiple_of(256 * at_t, 256), 256)]

        for name, tp, at_t, half in (
            ("right", right, t, None),
            ("left", left, t, None),
            ("twin", twin, t, None),
            ("far_right", right, left, 0),
            ("far_left", left, right, 1),
            ("twin_left", twin, left, None),
            ("twin_right", twin, right, None),
            ("twin_far0", twin, (t + 4) % NT, 0),
            ("twin_far1", twin, (t + 4) % NT, 1),
        ):
            bcopy[r, name] = copy(piece(at_t, half), piece(at_t, half), s, tp)

    def weight_half(step, turn):
        for way in (0, 1):
            h = way ^ turn
            wcopy[step, way, h].wait_recv()
            if (step + 1, way, h) in wcopy:
                go(wcopy[step + 1, way, h])

    def local_state(a, b, slot):
        for g in range(2):
            full = dot(a[:, GROUP * g : GROUP * (g + 1)], b[:, GROUP * g : GROUP * (g + 1)], 0, 0)
            kept = jnp.zeros((HDIM, GROUP), F32)
            for h in range(4):
                kept = kept + full[HDIM * h : HDIM * (h + 1), :] * head_mask(h, 0, GROUP)
            lstate[slot, HDIM * g : HDIM * (g + 1), :] = kept.astype(BF16)

    place = z % 4
    outward = jnp.where(place == 3, 1, -1)
    at_edge = (place == 0) | (place == 3)
    states = []
    for slot in (0, 1):
        first = [
            copy(
                lstate.at[slot, pl.ds(pl.multiple_of(QUARTER * ((y + d) % NY), 16), QUARTER)],
                lrecv.at[slot, y], along_y(d), t,
            )
            for d in range(1, NY)
        ]
        second = [
            copy(tsend.at[slot], trecv.at[slot, place], along_z((place + d) % 4 - place), t)
            for d in range(1, 4)
        ]
        edge = [copy(bsend.at[slot], brecv.at[slot], along_z(outward * d), t) for d in (1, 2)]
        third = [
            copy(
                pfs.at[slot, (y + d) % NY],
                state.at[slot, pl.ds(pl.multiple_of(QUARTER * y, 16), QUARTER)],
                along_y(d), t,
            )
            for d in range(1, NY)
        ]
        states.append((first, second, third, edge))

    def state_first(slot):
        for c in states[slot][0]:
            go(c)
        mine = pl.ds(pl.multiple_of(QUARTER * y, 16), QUARTER)
        lrecv[slot, y] = lstate[slot, mine, :]

    def state_second(slot):
        for c in states[slot][0]:
            c.wait_recv()
        total = lrecv[slot, 0].astype(F32)
        for j in range(1, NY):
            total = total + lrecv[slot, j].astype(F32)
        tsend[slot] = total.astype(BF16)
        for c in states[slot][1]:
            go(c)
        trecv[slot, place] = tsend[slot]

    def state_middle(slot):
        for c in states[slot][1]:
            c.wait_recv()
        before, total = jnp.zeros((QUARTER, GROUP), F32), jnp.zeros((QUARTER, GROUP), F32)
        for j in range(4):
            plane = trecv[slot, j].astype(F32)
            total = total + plane
            counts = j < place if slot == 0 else j > place
            before = before + jnp.where(counts, plane, 0.0)
        tacc[...] = before
        bsend[slot] = total.astype(BF16)

        @pl.when(at_edge & (z // 4 == slot))
        def _():
            for c in states[slot][3]:
                c.start()

    def state_third(slot):
        for i, near in enumerate((at_edge, jnp.logical_not(at_edge))):

            @pl.when(near & (z // 4 == 1 - slot))
            def _():
                states[slot][3][i].wait_recv()
                tacc[...] += brecv[slot].astype(F32)

        running = tacc[...]
        for j in range(NY) if slot == 0 else reversed(range(NY)):
            pfs[slot, j] = running.astype(BF16)
            running = running + lrecv[slot, j].astype(F32)
        for c in states[slot][2]:
            go(c)
        mine = pl.ds(pl.multiple_of(QUARTER * y, 16), QUARTER)
        state[slot, mine, :] = pfs[slot, y]

    def state_last(slot):
        for c in states[slot][2]:
            c.wait_recv()
        for g in range(2):
            compact = state[slot, HDIM * g : HDIM * (g + 1), :]
            for h in range(4):
                blocks[slot, g, HDIM * h : HDIM * (h + 1), :] = compact * head_mask(
                    h, 0, GROUP
                ).astype(BF16)

    sums = [
        [copy(ssend.at[i], srecv.at[i, d - 1], s, (t + d) % NT) for d in range(1, NT)]
        for i in range(2)
    ]

    def sum_send(i, column):
        ssend[i] = jnp.broadcast_to(column, (TOK, 128)).T[:8]
        for c in sums[i]:
            go(c)

    def sum_wait(i):
        total = ssend[i]
        for d in range(1, NT):
            sums[i][d - 1].wait_recv()
            total = total + srecv[i, d - 1]
        return jnp.broadcast_to(total[:1], (128, TOK)).T[:, :1]

    for c in loads:
        c.wait()
    local_state(k, v, 0)
    pl.semaphore_wait(barrier, len(peers))
    state_first(0)
    for way in (0, 1):
        go(wcopy[0, way, way])
    for d in range(1, NY):
        go(acopy[d])

    rows = lax.broadcasted_iota(jnp.int32, (TOK, TOK), 0)
    columns = lax.broadcasted_iota(jnp.int32, (TOK, TOK), 1)

    def lanes(g, lo, hi):
        return pl.ds(pl.multiple_of(GROUP * g + lo, 128), hi - lo)

    def forward(g):
        att[:, lanes(g, 0, GROUP)] = jnp.zeros((TOK, GROUP), F32)
        for h, (lo, hi) in enumerate(WINDOWS):
            mask = head_mask(h, lo, hi).astype(BF16)
            at = lanes(g, lo, hi)
            score = dot(q[:, at], k[:, at] * mask, 1, 1)
            score = jnp.where(rows >= columns, score, 0.0).astype(BF16)
            scores[4 * g + h] = score
            att[:, at] += dot(score, v[:, at] * mask, 1, 0)

    ncopy = {}
    for name, d, slot, first in (("up", 1, 3, 0), ("down", 3, 1, 1)):
        for turn, h in enumerate((first, 1 - first)):
            ncopy[name, turn] = copy(
                raw.at[pl.ds(128 * h, 128)], raw.at[pl.ds(TOK * slot + 128 * h, 128)],
                along_y(d), t,
            )
        ncopy[name, 2] = copy(
            raw.at[pl.ds(TOK * slot + 128 * first, 128)],
            raw.at[pl.ds(2 * TOK + 128 * first, 128)],
            along_y(d), t,
        )
    vcopy = [copy(vsend, vrecv.at[NY - d], along_y(d), t) for d in range(1, NY)]

    def turn_window(at_t):
        @pl.loop(1, NY)
        def _(r):
            block = grads[
                pl.ds(pl.multiple_of(TOK * r, TOK), TOK), pl.ds(pl.multiple_of(256 * at_t, 256), 256)
            ]
            turned[at_t, :, pl.ds(pl.multiple_of(TOK * r, TOK), TOK)] = block.T

    forward(0)
    state_second(0)
    for way in (0, 1):
        go(wcopy[0, way, 1 - way])
    weight_half(0, 0)
    state_middle(0)
    for d in range(1, NY):
        acopy[d].wait_recv()
        for name in ("right", "left", "twin"):
            go(bcopy[NY - d, name])
    forward(1)
    weight_half(0, 1)
    for c in own_grads:
        c.wait()

    @pl.loop(0, NZ)
    def _(j):
        turned[j, :, :TOK] = grads[:TOK, pl.ds(pl.multiple_of(256 * j, 256), 256)].T

    state_third(0)
    weight_half(1, 0)
    state_last(0)
    for g in range(2):
        at = lanes(g, 0, GROUP)
        att[:, at] += dot(q[:, at], blocks[0, g], 1, 0)
    raw[pl.ds(0, TOK), :] = att[...].astype(BF16)
    for turn in (0, 1):
        for name in ("up", "down"):
            go(ncopy[name, turn])
    sum_send(0, jnp.sum(att[...] * att[...], axis=1, keepdims=True))
    weight_half(1, 1)
    for r in range(1, NY):
        bcopy[r, "right"].wait_recv()
        go(bcopy[r, "far_right"])
        go(bcopy[r, "twin_left"])
        bcopy[r, "left"].wait_recv()
        go(bcopy[r, "far_left"])
        go(bcopy[r, "twin_right"])
    for at_t in (t, right, left):
        turn_window(at_t)
    weight_half(2, 0)
    for name in ("up", "down"):
        ncopy[name, 0].wait_recv()
        go(ncopy[name, 2])
    inverse = 1.0 / jnp.sqrt(sum_wait(0) / MODEL + EPSILON)
    vsend[...] = jnp.broadcast_to(inverse, (TOK, 128)).T[:8]
    for c in vcopy:
        go(c)
    weight_half(2, 1)
    for r in range(1, NY):
        bcopy[r, "far_right"].wait_recv()
        go(bcopy[r, "twin_far0"])
        bcopy[r, "far_left"].wait_recv()
        go(bcopy[r, "twin_far1"])
    for name in ("twin", "twin_left", "twin_right", "twin_far0", "twin_far1"):
        for r in range(1, NY):
            bcopy[r, name].wait_recv()
    for at_t in (twin, (twin + 2) % NT, (twin + 6) % NT, (t + 4) % NT, (twin + 4) % NT):
        turn_window(at_t)
    weight_half(3, 0)

    def product(r):
        @pl.loop(0, 3)
        def _(n):
            at = pl.ds(pl.multiple_of(256 * n, 256), 256)
            part[:, at] = dot(grads[pl.ds(TOK * r, TOK), :], weights[:, at], 1, 0)

    half_up = copy(hsend.at[pl.ds(0, 128)], hrecv.at[0], along_y(1), t)
    half_down = copy(hsend.at[pl.ds(128, 128)], hrecv.at[1], along_y(3), t)
    pcopy = {}
    for i, d in enumerate((1, 3)):
        for h in (0, 1):
            at = pl.ds(128 * h, 128)
            pcopy[i, h] = copy(psend.at[i, at], precv.at[i, at], along_y(d), t)

    def chunk(off):
        j = (z + off) % NZ

        @pl.loop(0, 3)
        def _(n):
            at = pl.ds(pl.multiple_of(256 * n, 256), 256)
            own[off, :, at] = dot(turned[j], normed[:, at], 1, 0)

    def valid(off, h):
        return own[off, pl.ds(pl.multiple_of(64 * odd + HALF * h, 32), HALF), :]

    dcopy = {}
    for step in range(4):
        for way in (0, 1):
            for h in (0, 1):
                if step > 0 or h == way:
                    at = pl.ds(HALF * h, HALF)
                    dcopy[step, way, h] = copy(
                        dsend.at[way, step, at], drecv.at[way, step, at],
                        along_z(2 * way - 1), t,
                    )

    def grad_half(step, turn):
        for way in (0, 1):
            h = way ^ (1 - turn)
            if (step, way, h) not in dcopy:
                continue
            off = 4 + step if way == 0 else 4 - step
            total = valid(off, h)
            if (step - 1, way, h) in dcopy:
                dcopy[step - 1, way, h].wait_recv()
                total = total + drecv[way, step - 1, HALF * h : HALF * (h + 1), :].astype(F32)
            dsend[way, step, HALF * h : HALF * (h + 1), :] = total.astype(BF16)
            go(dcopy[step, way, h])

    product(2)
    hsend[...] = part[...].astype(BF16)
    go(half_up)
    go(half_down)
    for name in ("up", "down"):
        ncopy[name, 1].wait_recv()
        ncopy[name, 2].wait_recv()
    for c in vcopy:
        c.wait_recv()
    for r in range(NY):
        at = pl.ds(TOK * r, TOK)
        if r == 0:
            normed[at, :] = (att[...] * inverse).astype(BF16)
        else:
            scale = jnp.broadcast_to(vrecv[r, :1], (128, TOK)).T[:, :1]
            normed[at, :] = (raw[at, :].astype(F32) * scale).astype(BF16)
    chunk(4)
    grad_half(0, 1)
    product(1)
    psend[0, 128:] = part[128:].astype(BF16)
    go(pcopy[0, 1])
    held[0] = part[:128]
    product(3)
    psend[1, :128] = part[:128].astype(BF16)
    go(pcopy[1, 0])
    held[1] = part[128:]

    @pl.loop(0, 2)
    def _(i):
        chunk(5 - 2 * i)

    grad_half(1, 0)
    half_up.wait_recv()
    psend[0, :128] = (held[0] + hrecv[0].astype(F32)).astype(BF16)
    go(pcopy[0, 0])
    half_down.wait_recv()
    psend[1, 128:] = (held[1] + hrecv[1].astype(F32)).astype(BF16)
    go(pcopy[1, 1])
    grad_half(1, 1)
    product(0)

    @pl.loop(0, 5)
    def _(i):
        e = i % 2
        chunk((1 - e) * ((6 + i // 2) % NZ) + e * (2 - i // 2))

    grad_half(2, 0)
    for c in pcopy.values():
        c.wait_recv()
    ng[...] = part[...] + precv[0].astype(F32) + precv[1].astype(F32)
    sum_send(1, jnp.sum(ng[...] * att[...], axis=1, keepdims=True))
    grad_half(2, 1)
    cross = sum_wait(1) * inverse
    grad_heads = (ng[...] - att[...] * (inverse * cross / MODEL)) * inverse
    gh[...] = grad_heads.astype(BF16)
    local_state(q, gh, 1)
    state_first(1)
    grad_half(3, 0)

    def backward(g):
        at = lanes(g, 0, GROUP)
        att[:, at] = dot(gh[:, at], blocks[0, g], 1, 1)
        part[:, at] = jnp.zeros((TOK, GROUP), F32)
        ng[:, at] = jnp.zeros((TOK, GROUP), F32)
        for h, (lo, hi) in enumerate(WINDOWS):
            mask = head_mask(h, lo, hi).astype(BF16)
            at = lanes(g, lo, hi)
            score = dot(gh[:, at], v[:, at] * mask, 1, 1)
            score = jnp.where(rows >= columns, score, 0.0).astype(BF16)
            att[:, at] += dot(score, k[:, at] * mask, 1, 0)
            part[:, at] += dot(score, q[:, at] * mask, 0, 0)
            ng[:, at] += dot(scores[4 * g + h], gh[:, at] * mask, 0, 0)

    backward(0)
    state_second(1)
    grad_half(3, 1)
    state_middle(1)
    backward(1)
    qg[...] = att[...].astype(BF16)
    state_third(1)
    state_last(1)
    for g in range(2):
        at = lanes(g, 0, GROUP)
        kg[:, at] = (part[:, at] + dot(v[:, at], blocks[1, g], 1, 1)).astype(BF16)
        vg[:, at] = (ng[:, at] + dot(k[:, at], blocks[1, g], 1, 0)).astype(BF16)
    for h in (0, 1):
        for way in (0, 1):
            dcopy[3, way, h].wait_recv()
        at = slice(HALF * h, HALF * (h + 1))
        total = valid(0, h) + drecv[0, 3, at, :].astype(F32) + drecv[1, 3, at, :].astype(F32)
        dw[at, :] = total.astype(BF16)

    for c in started:
        c.wait_send()
    for slot in (0, 1):

        @pl.when(at_edge & (z // 4 == slot))
        def _():
            for c in states[slot][3]:
                c.wait_send()


def deliver_kernel(*refs):
    sems = refs[-1]
    copies = [pltpu.make_async_copy(refs[i], refs[4 + i], sems.at[i]) for i in range(4)]
    for c in copies:
        c.start()
    for c in copies:
        c.wait()


def deliver(results):
    vmem = pl.BlockSpec(memory_space=pltpu.VMEM)
    return pl.pallas_call(
        deliver_kernel,
        out_shape=tuple(jax.ShapeDtypeStruct(x.shape, x.dtype) for x in results),
        in_specs=[vmem] * 4,
        out_specs=(pl.BlockSpec(memory_space=pl.ANY),) * 4,
        scratch_shapes=[pltpu.SemaphoreType.DMA((4,))],
    )(*results)


def body(q, k, v, og, w):
    vmem = pl.BlockSpec(memory_space=pltpu.VMEM)
    block = pltpu.VMEM((TOK, COLS), BF16)
    results = pl.pallas_call(
        kernel,
        out_shape=(block, block, block, pltpu.VMEM((CHUNK, COLS), BF16)),
        in_specs=[pl.BlockSpec(memory_space=pltpu.HBM)] * 5,
        out_specs=(vmem,) * 4,
        scratch_shapes=[
            pltpu.VMEM((TOK, COLS), BF16),
            pltpu.VMEM((TOK, COLS), BF16),
            pltpu.VMEM((TOK, COLS), BF16),
            pltpu.VMEM((NY * TOK, NZ * 256), BF16),
            pltpu.VMEM((NZ * 256, COLS), BF16),
            pltpu.VMEM((NY * TOK, COLS), BF16),
            pltpu.VMEM((8, TOK, TOK), BF16),
            pltpu.VMEM((TOK, COLS), F32),
            pltpu.VMEM((TOK, COLS), F32),
            pltpu.VMEM((TOK, COLS), F32),
            pltpu.VMEM((2, TOK, COLS), BF16),
            pltpu.VMEM((2, TOK, COLS), BF16),
            pltpu.VMEM((TOK, COLS), BF16),
            pltpu.VMEM((2, 128, COLS), BF16),
            pltpu.VMEM((2, 192, GROUP), BF16),
            pltpu.VMEM((2, NY, QUARTER, GROUP), BF16),
            pltpu.VMEM((2, QUARTER, GROUP), BF16),
            pltpu.VMEM((2, 4, QUARTER, GROUP), BF16),
            pltpu.VMEM((2, QUARTER, GROUP), BF16),
            pltpu.VMEM((2, QUARTER, GROUP), BF16),
            pltpu.VMEM((QUARTER, GROUP), F32),
            pltpu.VMEM((2, NY, QUARTER, GROUP), BF16),
            pltpu.VMEM((2, 192, GROUP), BF16),
            pltpu.VMEM((2, 2, GROUP, GROUP), BF16),
            pltpu.VMEM((2, 8, TOK), F32),
            pltpu.VMEM((2, NT - 1, 8, TOK), F32),
            pltpu.VMEM((NZ, 256, COLS), F32),
            pltpu.VMEM((2, 4, CHUNK, COLS), BF16),
            pltpu.VMEM((2, 4, CHUNK, COLS), BF16),
            pltpu.VMEM((NZ, 256, NY * TOK), BF16),
            pltpu.VMEM((TOK, COLS), BF16),
            pltpu.VMEM((2, 128, COLS), F32),
            pltpu.VMEM((NY * TOK, COLS), BF16),
            pltpu.VMEM((8, TOK), F32),
            pltpu.VMEM((NY, 8, TOK), F32),
            pltpu.SemaphoreType.DMA((SEMS,)),
            pltpu.SemaphoreType.DMA((SEMS,)),
            pltpu.SemaphoreType.DMA((NZ + 4,)),
        ],
        compiler_params=pltpu.CompilerParams(
            collective_id=0, has_side_effects=True, vmem_limit_bytes=56 << 20
        ),
    )(q, k, v, w.T, og)
    *grads, weight_grad = deliver([pltpu.with_memory_space_constraint(x, pltpu.VMEM) for x in results])
    return *grads, weight_grad.T


def solution(mesh):
    placed = (P("seq", "tp"), P("seq", "tp"), P("seq", "tp"), P("seq", None), P("tp", "seq"))
    return jax.shard_map(
        body,
        mesh=mesh,
        in_specs=placed,
        out_specs=(P("seq", "tp"), P("seq", "tp"), P("seq", "tp"), P("tp", "seq")),
        check_vma=False,
    )
```
